32 devices in a mesh: shot: 4 (over y, x), gx: 2 (over core), gy: 4 (over z).
Axes of the slice: x: 2, y: 2, z: 4, core: 2. Of those that a mesh axis runs over, the one named last changes fastest.
Arguments:
- fwd_now: float32 [8, 32, 128, 256], P('shot', 'gx', 'gy'), may hold values from -6 to 6
- fwd_next: float32 [8, 32, 128, 256], P('shot', 'gx', 'gy'), may hold values from -6 to 6
- adj_now: float32 [8, 32, 128, 256], P('shot', 'gx', 'gy'), may hold values from -6 to 6
- adj_next: float32 [8, 32, 128, 256], P('shot', 'gx', 'gy'), may hold values from -6 to 6
- courant: float32 [32, 128, 256], P('gx', 'gy'), may hold values from 0.15 to 0.45
- wavelet: float32 [8, 128], P('shot'), may hold values from -24 to 24
- traces: float32 [8, 128, 1024], P('shot'), may hold values from -6 to 6
- src_cells: int32 [8], P('shot'), may hold values from 0 to 4095
- rec_cells: int32 [8, 1024], P('shot'), may hold values from 0 to 4095
- step_index: int32 [8], P('shot'), may hold values from 1 to 127
Outputs:
- forward_prior: float32 [8, 32, 128, 256], P('shot', 'gx', 'gy')
- forward_start: float32 [8, 32, 128, 256], P('shot', 'gx', 'gy')
- adjoint_prior: float32 [8, 32, 128, 256], P('shot', 'gx', 'gy')
- adjoint_start: float32 [8, 32, 128, 256], P('shot', 'gx', 'gy')
- gradient: float32 [32, 128, 256], P('gx', 'gy', 'shot')
The draws below stay inside these ranges and needn't reach their ends.
Inputs may be any that keep to these rules, and one draw needn't show every extreme that they name: `src_cells`: a horizontal cell x * 128 + y of the grid. `rec_cells`: a horizontal cell x * 128 + y of the grid; several receivers may share a cell. `step_index`: a time step k such that the samples k and k - 1 exist (k ≥ 1).
All inputs are finite; a program needn't handle non-finite values.
Results may differ from the reference program's by a relative error of at most 0.0003.
Values sent between devices are 32-bit elements; how exact they have to be, the bound alone decides.
No kernel may reach another device: no remote copies, remote signals or barrier semaphores. Data moves between devices by JAX's collectives and lax.ppermute only.
A program may use at most 64 MiB of HBM per device.

```python
import jax
import jax.numpy as jnp
from jax import lax

NZ = 256
SHOT_DEV = 2
STEPS = 2
NT = 128
NREC = 1024
SRC_DEPTH = 4
REC_DEPTH = 6
SHOTS = 8
NX = 32
NY = 128


def wave_field(key, offset, spiked):
    subkeys = jax.random.split(jax.random.fold_in(key, offset), 2)
    values = jax.random.normal(subkeys[0], (SHOTS, NX, NY, NZ), jnp.float32)
    if spiked:
        groups = SHOTS // SHOT_DEV
        paired = jax.random.permutation(subkeys[1], groups)
        shot_group = jnp.arange(SHOTS, dtype=jnp.int32) // SHOT_DEV
        depth_block = jnp.arange(NZ, dtype=jnp.int32) // (NZ // groups)
        chosen = paired[shot_group][:, None] == depth_block[None, :]
        values = values * jnp.where(chosen, 2.5, 1.0)[:, None, None, :]
    return jnp.clip(values, -6.0, 6.0)


def draw_fwd_now(key, part):
    return wave_field(key, 11, False)


def draw_fwd_next(key, part):
    return wave_field(key, 12, False)


def draw_adj_now(key, part):
    return wave_field(key, 13, True)


def draw_adj_next(key, part):
    return wave_field(key, 14, False)


def draw_wavelet(key, part):
    tagged = jax.random.fold_in(key, 15)
    return jnp.clip(4.0 * jax.random.normal(tagged, (SHOTS, NT), jnp.float32), -24.0, 24.0)


def with_ends(array, own_key, low, top_value):
    index_at = [jax.random.randint(jax.random.fold_in(own_key, axis), (), 0, length) for axis, length in enumerate(array.shape)]
    widest = array.shape.index(max(array.shape))
    next_to = index_at[:widest] + [(index_at[widest] + 1) % array.shape[widest]] + index_at[widest + 1:]
    return array.at[tuple(index_at)].set(low).at[tuple(next_to)].set(top_value)


def block_scale(stream_key, shape, cuts, low, high):
    gain, own = 1.0, jax.random.fold_in(stream_key, 6)
    for dim, shards_of in cuts:
        heights = jnp.exp(jax.random.uniform(jax.random.fold_in(own, dim), (shards_of,), jnp.float32, low / len(cuts), high / len(cuts)))
        gain = gain * jnp.repeat(heights, shape[dim] // shards_of).reshape([-1 if axis == dim else 1 for axis in range(len(shape))])
    return gain


def normal_values(stream_key, extent, width, most, pieces=(), kind=jnp.bfloat16):
    result = width * jax.random.normal(stream_key, extent, jnp.float32)
    if pieces:
        result = result * block_scale(stream_key, extent, pieces, -0.22, 0.18)
    return jnp.clip(result, -most, most).astype(kind)


def setup_inputs(seed: int = 0) -> dict:
    arg_keys = jax.random.split(jax.random.key(seed), 11)
    return {
        "fwd_now": draw_fwd_now(jax.random.fold_in(arg_keys[10], 71), 0),
        "fwd_next": draw_fwd_next(jax.random.fold_in(arg_keys[10], 71), 0),
        "adj_now": draw_adj_now(jax.random.fold_in(arg_keys[10], 71), 0),
        "adj_next": draw_adj_next(jax.random.fold_in(arg_keys[10], 71), 0),
        "courant": jnp.clip(0.15 + 0.29999998 * jax.random.uniform(arg_keys[4], (NX, NY, NZ), jnp.float32) ** block_scale(arg_keys[4], (NX, NY, NZ), ((0, 2), (1, 4)), -0.2, 0.2), 0.15, 0.45),
        "wavelet": draw_wavelet(jax.random.fold_in(arg_keys[10], 71), 0),
        "traces": normal_values(arg_keys[6], (SHOTS, NT, NREC), 1.0, 6.0, ((0, 4),), jnp.float32),
        "src_cells": with_ends(jax.random.randint(arg_keys[7], (SHOTS,), 0, NX * NY), jax.random.fold_in(arg_keys[7], 1), 0, (NX * NY) - 1).astype(jnp.int32),
        "rec_cells": with_ends(jax.random.randint(arg_keys[8], (SHOTS, NREC), 0, NX * NY), jax.random.fold_in(arg_keys[8], 1), 0, (NX * NY) - 1).astype(jnp.int32),
        "step_index": with_ends(jax.random.randint(arg_keys[9], (SHOTS,), STEPS - 1, NT), jax.random.fold_in(arg_keys[9], 1), STEPS - 1, NT - 1).astype(jnp.int32),
    }


COEFS = (-205.0 / 72.0, 8.0 / 5.0, -1.0 / 5.0, 8.0 / 315.0, -1.0 / 560.0)


def laplace(field):
    size_x, size_y, size_z = field.shape
    padded = jnp.pad(field, 4)
    total = 3.0 * COEFS[0] * field
    for reach in range(1, 5):
        part = padded[4 + reach:4 + reach + size_x, 4:4 + size_y, 4:4 + size_z] + padded[4 - reach:4 - reach + size_x, 4:4 + size_y, 4:4 + size_z]
        part = part + padded[4:4 + size_x, 4 + reach:4 + reach + size_y, 4:4 + size_z] + padded[4:4 + size_x, 4 - reach:4 - reach + size_y, 4:4 + size_z]
        part = part + padded[4:4 + size_x, 4:4 + size_y, 4 + reach:4 + reach + size_z] + padded[4:4 + size_x, 4:4 + size_y, 4 - reach:4 - reach + size_z]
        total = total + COEFS[reach] * part
    return total


def reference(fwd_now, fwd_next, adj_now, adj_next, courant, wavelet, traces, src_cells, rec_cells, step_index):
    mass = courant * courant
    cells_x = jnp.arange(NX, dtype=jnp.int32)[:, None, None]
    cells_y = jnp.arange(NY, dtype=jnp.int32)[None, :, None]
    cells_z = jnp.arange(NZ, dtype=jnp.int32)[None, None, :]

    def one_shot(image, items):
        u_now, u_next, a_now, a_next, wave, trace, source_cell, receivers, step = items
        mask = (cells_x == source_cell // NY) & (cells_y == source_cell % NY) & (cells_z == SRC_DEPTH)
        slots = ((receivers // NY) * NY + receivers % NY) * NZ + REC_DEPTH
        for offset in range(STEPS):
            moment = (step - offset).astype(jnp.int32)
            lap_u = laplace(u_now)
            lap_a = laplace(mass * a_now)
            image = image + a_now * lap_u
            sample = lax.dynamic_index_in_dim(wave, moment, 0, keepdims=False)
            u_prev = 2.0 * u_now - u_next + mass * (lap_u + jnp.where(mask, sample, 0.0))
            values = lax.dynamic_index_in_dim(trace, moment, 0, keepdims=False)
            inject = jnp.zeros((NX * NY * NZ,), u_now.dtype).at[slots].add(values).reshape(NX, NY, NZ)
            a_prev = 2.0 * a_now - a_next + lap_a + inject
            u_next, u_now = u_now, u_prev
            a_next, a_now = a_now, a_prev
        return image, (u_next, u_now, a_next, a_now)

    start = jnp.zeros((NX, NY, NZ), courant.dtype)
    image, states = lax.scan(one_shot, start, (fwd_now, fwd_next, adj_now, adj_next, wavelet, traces, src_cells, rec_cells, step_index))
    gradient = 2.0 * courant * image / (SHOTS * STEPS)
    return states[0], states[1], states[2], states[3], gradient
```

```python
import functools

import jax
import jax.numpy as jnp
from jax import lax
from jax.experimental import pallas as pl
from jax.experimental.pallas import tpu as pltpu
from jax.sharding import PartitionSpec as P

STEPS = 2
SRC_DEPTH = 4
REC_DEPTH = 6
COEFS = (-205.0 / 72.0, 8.0 / 5.0, -1.0 / 5.0, 8.0 / 315.0, -1.0 / 560.0)
F32 = jnp.float32
VMEM = pl.BlockSpec(memory_space=pltpu.VMEM)
SMEM = pl.BlockSpec(memory_space=pltpu.SMEM)
ANY = pl.BlockSpec(memory_space=pl.ANY)


def iota(dim):
    return lax.broadcasted_iota(jnp.int32, (8, 128), dim)


def even_on(axis):
    return lax.axis_index(axis) % 2 == 0


def pair_permutes(axis):
    count = lax.axis_size(axis)
    perms = []
    for first in (0, 1):
        pairs = [(i, i + 1) for i in range(first, count - 1, 2)]
        if pairs:
            perms.append(pairs + [(b, a) for a, b in pairs])
    return perms


def edge_layer(axis, width, turn, k):
    high = even_on(axis) if turn == 0 else jnp.logical_not(even_on(axis))
    return jnp.where(high, width - 1 - k, k)


def halves(depth):
    return [slice(h * 128, h * 128 + 128) for h in range(depth // 128)]


def write_y_sends(sends, s, x, z, u_low, m_low, u_high, m_high):
    sub = iota(0)
    low = jnp.where(sub < 4, u_low, pltpu.roll(m_low, 4, 0))
    high = jnp.where(sub < 4, pltpu.roll(u_high, 4, 0), m_high)
    even = even_on("gy")
    for turn, ref in enumerate(sends):
        pick = even if turn == 0 else jnp.logical_not(even)
        ref[s, x, :, z] = jnp.where(pick, high, low)


def first_sends(turns_x, turns_y, u_hbm, a_hbm, c_hbm, *refs):
    ys, refs = refs[:turns_y], refs[turns_y:]
    xs, refs = refs[:turns_x], refs[turns_x:]
    u_low, u_high, a_low, a_high, c_low, c_high, u_x, a_x, c_x, sems = refs
    shots, width_x, width_y, depth = u_hbm.shape
    copies = []

    def fetch(src, dst):
        copy = pltpu.make_async_copy(src, dst, sems.at[len(copies)])
        copy.start()
        copies.append(copy)

    for src, low, high in ((u_hbm, u_low, u_high), (a_hbm, a_low, a_high)):
        fetch(src.at[:, :, 0:8, :], low)
        fetch(src.at[:, :, width_y - 8 : width_y, :], high)
    fetch(c_hbm.at[:, 0:8, :], c_low)
    fetch(c_hbm.at[:, width_y - 8 : width_y, :], c_high)
    for turn in range(turns_x):
        first = jnp.minimum(
            edge_layer("gx", width_x, turn, 0), edge_layer("gx", width_x, turn, 3)
        )
        fetch(u_hbm.at[:, pl.ds(first, 4)], u_x.at[turn])
        fetch(a_hbm.at[:, pl.ds(first, 4)], a_x.at[turn])
        fetch(c_hbm.at[pl.ds(first, 4)], c_x.at[turn])
    for copy in copies:
        copy.wait()

    def line(x, carry):
        for z in halves(depth):
            mass_low = c_low[x, :, z] * c_low[x, :, z]
            mass_high = c_high[x, :, z] * c_high[x, :, z]
            for s in range(shots):
                write_y_sends(
                    ys,
                    s,
                    x,
                    z,
                    u_low[s, x, :, z],
                    mass_low * a_low[s, x, :, z],
                    u_high[s, x, :, z],
                    mass_high * a_high[s, x, :, z],
                )
        return carry

    lax.fori_loop(0, width_x, line, 0)
    for turn in range(turns_x):
        top = edge_layer("gx", width_x, turn, 0) > 3
        for k in range(4):
            layer = jnp.where(top, 3 - k, k)
            mass = c_x[turn, layer] * c_x[turn, layer]
            for s in range(shots):
                xs[turn][0, s, k] = u_x[turn, s, layer]
                xs[turn][1, s, k] = mass * a_x[turn, s, layer]


def laplace_tile(field, s, x, row):
    lane = iota(1)
    center = [field[s, h, x + 4, pl.ds(row, 8), :] for h in range(2)]
    total = [3.0 * COEFS[0] * c for c in center]
    for r in range(1, 5):
        right = [pltpu.roll(c, r, 1) for c in center]
        left = [pltpu.roll(c, 128 - r, 1) for c in center]
        low, high = lane < r, lane >= 128 - r
        deep = [
            jnp.where(low, 0.0, right[0]) + jnp.where(high, left[1], left[0]),
            jnp.where(low, right[0], right[1]) + jnp.where(high, 0.0, left[1]),
        ]
        for h in range(2):
            part = field[s, h, x + 4 + r, pl.ds(row, 8), :] + field[s, h, x + 4 - r, pl.ds(row, 8), :]
            part = part + field[s, h, x + 4, pl.ds(row + r, 8), :] + field[s, h, x + 4, pl.ds(row - r, 8), :]
            total[h] = total[h] + COEFS[r] * (part + deep[h])
    return center, total


def march(offset, rows_y, step_ref, src_ref, wave_ref, rec_ref, trace_hbm, u, u_old, a, a_old, cour, *refs):
    image_in, refs = (refs[0], refs[1:]) if offset else (None, refs)
    u_out, a_out, image, field_u, field_m, trace, sems = refs
    shots, width_x, width_y, depth = u.shape
    tiles = width_y // 8
    copies = []
    for s in range(shots):
        moment = step_ref[s] - offset
        block = pl.multiple_of((moment // 8) * 8, 8)
        copy = pltpu.make_async_copy(trace_hbm.at[s, pl.ds(block, 8), :], trace.at[s], sems.at[s])
        copy.start()
        copies.append(copy)
    zero = jnp.zeros((8, 128), F32)
    for field in (field_u, field_m):
        for s in range(shots):
            for h in range(2):
                for x in (0, 1, 2, 3, width_x + 4, width_x + 5, width_x + 6, width_x + 7):
                    for t in range(1, tiles + 1):
                        field[s, h, x, 8 * t : 8 * t + 8, :] = zero

    def fill(x, carry):
        for h, z in enumerate(halves(depth)):
            for t in range(tiles):
                row = slice(8 * t, 8 * t + 8)
                mass = cour[x, row, z] * cour[x, row, z]
                for s in range(shots):
                    field_u[s, h, x + 4, 8 * t + 8 : 8 * t + 16, :] = u[s, x, row, z]
                    field_m[s, h, x + 4, 8 * t + 8 : 8 * t + 16, :] = mass * a[s, x, row, z]
            for field in (field_u, field_m):
                for s in range(shots):
                    field[s, h, x + 4, 0:8, :] = zero
                    field[s, h, x + 4, width_y + 8 : width_y + 16, :] = zero
        return carry

    lax.fori_loop(0, width_x, fill, 0)

    def line(x, carry):
        for t in range(tiles):
            row = slice(8 * t, 8 * t + 8)
            mass = [cour[x, row, z] * cour[x, row, z] for z in halves(depth)]
            terms = [image_in[h, x, row, :] if offset else None for h in range(2)]
            for s in range(shots):
                center, lap_u = laplace_tile(field_u, s, x, 8 * t + 8)
                _, lap_a = laplace_tile(field_m, s, x, 8 * t + 8)
                for h, z in enumerate(halves(depth)):
                    a_now = a[s, x, row, z]
                    term = a_now * lap_u[h]
                    terms[h] = term if terms[h] is None else terms[h] + term
                    u_out[s, x, row, z] = 2.0 * center[h] - u_old[s, x, row, z] + mass[h] * lap_u[h]
                    a_out[s, x, row, z] = 2.0 * a_now - a_old[s, x, row, z] + lap_a[h]
            for h in range(2):
                image[h, x, row, :] = terms[h]
        return carry

    lax.fori_loop(0, width_x, line, 0)

    bits = rows_y.bit_length() - 1
    anchor_x = lax.axis_index("gx") * width_x
    anchor_y = lax.axis_index("gy") * width_y
    lane, sub = iota(1), iota(0)
    for s in range(shots):
        moment = step_ref[s] - offset
        place_x = lax.shift_right_logical(src_ref[s], bits) - anchor_x
        place_y = (src_ref[s] & (rows_y - 1)) - anchor_y
        here = (place_x >= 0) & (place_x < width_x) & (place_y >= 0) & (place_y < width_y)

        @pl.when(here)
        def _():
            row = pl.ds(pl.multiple_of((place_y // 8) * 8, 8), 8)
            speed = cour[place_x, row, 0:128]
            hit = (sub == place_y % 8) & (lane == SRC_DEPTH)
            added = jnp.where(hit, speed * speed * wave_ref[s, moment], 0.0)
            u_out[s, place_x, row, 0:128] = u_out[s, place_x, row, 0:128] + added

        copies[s].wait()
        pick = lax.broadcasted_iota(jnp.int32, trace.shape[1:], 0) == moment % 8
        values = jnp.sum(jnp.where(pick, trace[s], 0.0), axis=0, keepdims=True)
        cells = rec_ref[s : s + 1, :]
        count = cells.shape[1]
        cell_x = lax.shift_right_logical(cells, bits) - anchor_x
        cell_y = (cells & (rows_y - 1)) - anchor_y
        hot_x = lax.broadcasted_iota(jnp.int32, (width_x, count), 0) == cell_x
        hot_y = lax.broadcasted_iota(jnp.int32, (width_y, count), 0) == cell_y
        plane = lax.dot_general(
            jnp.where(hot_y, values, 0.0),
            jnp.where(hot_x, 1.0, 0.0),
            (((1,), (1,)), ((), ())),
            precision=lax.Precision.HIGHEST,
            preferred_element_type=F32,
        )
        depth_mask = lax.broadcasted_iota(jnp.int32, (width_y, 128), 1) == REC_DEPTH
        for x in range(width_x):
            added = jnp.where(depth_mask, plane[:, x : x + 1], 0.0)
            a_out[s, x, :, 0:128] = a_out[s, x, :, 0:128] + added


def packed(load, target, x):
    lane = lax.broadcasted_iota(jnp.int32, (16, 128), 1)
    block = load(target // 2, x)
    top, bottom = block[0:16, :], block[16:32, :]
    front = jnp.where(lane < 64, top, pltpu.roll(bottom, 64, 1))
    back = jnp.where(lane < 64, pltpu.roll(top, 64, 1), bottom)
    return jnp.where(target % 2 == 0, front, back)


def edge(turns_x, turns_y, last, *refs):
    hy, refs = refs[:turns_y], refs[turns_y:]
    hx, refs = refs[:turns_x], refs[turns_x:]
    a, cour, u_in, a_in, image_in, u_out, a_out, image, *sends = refs
    shots, width_x, width_y, depth = a.shape
    sub = iota(0)
    even = even_on("gy")

    def keep(x, carry):
        for s in range(shots):
            u_out[s, x] = u_in[s, x]
            a_out[s, x] = a_in[s, x]
        for h in range(2):
            image[h, x] = image_in[h, x]
        return carry

    lax.fori_loop(0, width_x, keep, 0)

    def coef(values):
        out = jnp.zeros((8, 128), F32)
        for j, v in values:
            out = jnp.where(sub == j, v, out)
        return out

    low_coef = [None] + [coef([(j, COEFS[r]) for j in range(4) if j < r]) for r in range(1, 5)]
    high_coef = [None] + [coef([(p, COEFS[r]) for p in range(4, 8) if p >= 8 - r]) for r in range(1, 5)]

    def turned(v, shift):
        return v if shift % 8 == 0 else pltpu.roll(v, shift % 8, 0)

    def rows(x, carry):
        for h, z in enumerate(halves(depth)):
            terms = [image[h, x, 0:8, :], image[h, x, width_y - 8 : width_y, :]]
            for s in range(shots):
                first = hy[0][s, x, :, z]
                second = hy[1][s, x, :, z] if turns_y > 1 else jnp.zeros_like(first)
                below = jnp.where(even, second, first)
                above = jnp.where(even, first, second)
                for side in range(2):
                    row = slice(0, 8) if side == 0 else slice(width_y - 8, width_y)
                    lap_u = lap_a = None
                    for r in range(1, 5):
                        if side == 0:
                            part_u = low_coef[r] * turned(below, r - 4)
                            part_a = low_coef[r] * turned(below, r)
                        else:
                            part_u = high_coef[r] * turned(above, 8 - r)
                            part_a = high_coef[r] * turned(above, 4 - r)
                        lap_u = part_u if lap_u is None else lap_u + part_u
                        lap_a = part_a if lap_a is None else lap_a + part_a
                    mass = cour[x, row, z] * cour[x, row, z]
                    u_out[s, x, row, z] = u_out[s, x, row, z] + mass * lap_u
                    a_out[s, x, row, z] = a_out[s, x, row, z] + lap_a
                    terms[side] = terms[side] + a[s, x, row, z] * lap_u
            image[h, x, 0:8, :] = terms[0]
            image[h, x, width_y - 8 : width_y, :] = terms[1]
        return carry

    lax.fori_loop(0, width_x, rows, 0)
    for turn in range(turns_x):
        for j in range(4):
            x = edge_layer("gx", width_x, turn, j)
            for h, z in enumerate(halves(depth)):
                term = image[h, x]
                for s in range(shots):
                    lap_u = lap_a = None
                    for k in range(4 - j):
                        part_u = COEFS[j + k + 1] * hx[turn][0, s, k, :, z]
                        part_a = COEFS[j + k + 1] * hx[turn][1, s, k, :, z]
                        lap_u = part_u if lap_u is None else lap_u + part_u
                        lap_a = part_a if lap_a is None else lap_a + part_a
                    mass = cour[x, :, z] * cour[x, :, z]
                    u_out[s, x, :, z] = u_out[s, x, :, z] + mass * lap_u
                    a_out[s, x, :, z] = a_out[s, x, :, z] + lap_a
                    term = term + a[s, x, :, z] * lap_u
                image[h, x] = term
    if last:
        me = lax.axis_index("shot")

        def parts(x, carry):
            for k, ref in enumerate(sends):
                ref[x] = packed(lambda h, x: image[h, x], me ^ k, x)
            return carry

        lax.fori_loop(0, width_x, parts, 0)
        return
    ys, xs = sends[:turns_y], sends[turns_y:]

    def outgoing(x, carry):
        for z in halves(depth):
            tile = []
            for row in (slice(0, 8), slice(width_y - 8, width_y)):
                mass = cour[x, row, z] * cour[x, row, z]
                tile.append((row, mass))
            for s in range(shots):
                (low, mass_low), (high, mass_high) = tile
                write_y_sends(
                    ys,
                    s,
                    x,
                    z,
                    u_out[s, x, low, z],
                    mass_low * a_out[s, x, low, z],
                    u_out[s, x, high, z],
                    mass_high * a_out[s, x, high, z],
                )
        return carry

    lax.fori_loop(0, width_x, outgoing, 0)
    for turn in range(turns_x):
        for k in range(4):
            x = edge_layer("gx", width_x, turn, k)
            mass = cour[x] * cour[x]
            for s in range(shots):
                xs[turn][0, s, k] = u_out[s, x]
                xs[turn][1, s, k] = mass * a_out[s, x]


def finish(scale, cour, own, first, second, third, out):
    me = lax.axis_index("shot")

    def line(x, carry):
        speed = packed(lambda h, x: jnp.where(h == 0, cour[x, :, 0:128], cour[x, :, 128:256]), me, x)
        total = own[x] + first[x] + second[x] + third[x]
        value = 2.0 * speed * total / scale
        out[x, 0:16, :] = value[:, 0:64]
        out[x, 16:32, :] = value[:, 64:128]
        return carry

    lax.fori_loop(0, out.shape[0], line, 0)


def call(body, name, outs, scratch, in_specs, args, cost, limit=40 << 20):
    return pl.pallas_call(
        body,
        name=name,
        out_shape=outs,
        in_specs=in_specs,
        out_specs=[VMEM] * len(outs),
        scratch_shapes=scratch,
        compiler_params=pltpu.CompilerParams(vmem_limit_bytes=limit),
        cost_estimate=pl.CostEstimate(flops=cost, bytes_accessed=cost, transcendentals=0),
    )(*args)


def shards(
    fwd_now, fwd_next, adj_now, adj_next, courant, wavelet, traces, src_cells, rec_cells, step_index
):
    shots, width_x, width_y, depth = fwd_now.shape
    groups = lax.axis_size("shot")
    rows_y = width_y * lax.axis_size("gy")
    assert rows_y & (rows_y - 1) == 0 and depth == 256 and groups == 4 and width_y == 32
    perms_x, perms_y = pair_permutes("gx"), pair_permutes("gy")
    turns_x, turns_y = len(perms_x), len(perms_y)

    def shape(*dims):
        return jax.ShapeDtypeStruct(dims, F32)

    y_send, x_send = (shots, width_x, 8, depth), (2, shots, 4, width_y, depth)
    send_shapes = [shape(*y_send)] * turns_y + [shape(*x_send)] * turns_x
    y_rows, x_rows = (shots, width_x, 8, depth), (turns_x, shots, 4, width_y, depth)
    scratch = [pltpu.VMEM(y_rows, F32)] * 4 + [pltpu.VMEM(y_rows[1:], F32)] * 2
    scratch += [pltpu.VMEM(x_rows, F32)] * 2 + [pltpu.VMEM((turns_x, 4, width_y, depth), F32)]
    scratch += [pltpu.SemaphoreType.DMA((6 + 3 * turns_x,))]
    sends = call(
        functools.partial(first_sends, turns_x, turns_y),
        "first_sends",
        send_shapes,
        scratch,
        [ANY] * 3,
        (fwd_now, adj_now, courant),
        1 << 20,
    )
    u_now, u_next, a_now, a_next = fwd_now, fwd_next, adj_now, adj_next
    image = None
    for offset in range(STEPS):
        last = offset == STEPS - 1
        halo_y = [lax.ppermute(s, "gy", p) for s, p in zip(sends[:turns_y], perms_y)]
        halo_x = [lax.ppermute(s, "gx", p) for s, p in zip(sends[turns_y:], perms_x)]
        padded = pltpu.VMEM((shots, 2, width_x + 8, width_y + 16, 128), F32)
        args = (step_index, src_cells, wavelet, rec_cells, traces, u_now, u_next, a_now, a_next, courant)
        args += (image,) if offset else ()
        state = [shape(*fwd_now.shape)] * 2 + [shape(2, width_x, width_y, 128)]
        u_prev, a_prev, image = call(
            functools.partial(march, offset, rows_y),
            f"march_{offset}",
            state,
            [padded, padded, pltpu.VMEM((shots, 8, traces.shape[-1]), F32), pltpu.SemaphoreType.DMA((shots,))],
            [SMEM] * 3 + [VMEM, ANY] + [VMEM] * (len(args) - 5),
            args,
            16 << 20,
        )
        args = (*halo_y, *halo_x, a_now, courant, u_prev, a_prev, image)
        outs = state + ([shape(width_x, 16, 128)] * groups if last else send_shapes)
        u_prev, a_prev, image, *sends = call(
            functools.partial(edge, turns_x, turns_y, last),
            f"edge_{offset}",
            outs,
            [],
            [VMEM] * len(args),
            args,
            2 << 20,
        )
        u_next, u_now = u_now, u_prev
        a_next, a_now = a_now, a_prev
    parts = [sends[0]]
    for k in range(1, groups):
        parts.append(lax.ppermute(sends[k], "shot", [(i, i ^ k) for i in range(groups)]))
    (gradient,) = call(
        functools.partial(finish, float(shots * groups * STEPS)),
        "finish",
        [shape(width_x, width_y, depth // groups)],
        [],
        [VMEM] * 5,
        (courant, *parts),
        1 << 20,
    )
    return (u_next, u_now, a_next, a_now, gradient)


def solution(mesh):
    fields = P("shot", "gx", "gy", None)
    in_specs = (fields,) * 4 + (
        P("gx", "gy", None),
        P("shot", None),
        P("shot", None, None),
        P("shot"),
        P("shot", None),
        P("shot"),
    )
    out_specs = (fields,) * 4 + (P("gx", "gy", "shot"),)
    return jax.shard_map(shards, mesh=mesh, in_specs=in_specs, out_specs=out_specs, check_vma=False)
```

```python
import functools

import jax
import jax.numpy as jnp
from jax import lax
from jax.experimental import pallas as pl
from jax.experimental.pallas import tpu as pltpu
from jax.sharding import PartitionSpec as P

STEPS = 2
SRC_DEPTH = 4
REC_DEPTH = 6
COEFS = (-205.0 / 72.0, 8.0 / 5.0, -1.0 / 5.0, 8.0 / 315.0, -1.0 / 560.0)
F32 = jnp.float32
BF16 = jnp.bfloat16
VMEM = pl.BlockSpec(memory_space=pltpu.VMEM)
SMEM = pl.BlockSpec(memory_space=pltpu.SMEM)
HBM = pl.BlockSpec(memory_space=pltpu.HBM)


def iota(dim):
    return lax.broadcasted_iota(jnp.int32, (8, 128), dim)


def even_on(axis):
    return lax.axis_index(axis) % 2 == 0


def pair_permutes(axis, other):
    count, across = lax.axis_size(axis), lax.axis_size(other)
    perms = []

    def at(i, j):
        return i * across + j if axis == "gx" else j * count + i

    for first in (0, 1):
        pairs = [(i, i + 1) for i in range(first, count - 1, 2)]
        if not pairs:
            continue
        left = set(range(count)) - {i for pair in pairs for i in pair}
        perm = [(at(a, j), at(b, j)) for a, b in pairs for j in range(across)]
        perm += [(b, a) for a, b in perm]
        if across % 2 == 0:
            perm += [(at(i, j), at(i, j ^ 1)) for i in sorted(left) for j in range(across)]
        perms.append(perm)
    return perms


def has_neighbour(axis, step):
    at = lax.axis_index(axis) + step
    return (at >= 0) & (at < lax.axis_size(axis))


def edge_layer(axis, width, turn, k):
    high = even_on(axis) if turn == 0 else jnp.logical_not(even_on(axis))
    return jnp.where(high, width - 1 - k, k)


def in_hbm(x):
    return pltpu.with_memory_space_constraint(x, pltpu.HBM)


def in_vmem(x):
    return pltpu.with_memory_space_constraint(x, pltpu.VMEM)


def halves(depth):
    return [slice(h * 128, h * 128 + 128) for h in range(depth // 128)]


def write_y_sends(sends, s, x, z, u_low, m_low, u_high, m_high):
    sub = iota(0)
    low = jnp.where(sub < 4, u_low, pltpu.roll(m_low, 4, 0))
    high = jnp.where(sub < 4, pltpu.roll(u_high, 4, 0), m_high)
    even = even_on("gy")
    for turn, ref in enumerate(sends):
        pick = even if turn == 0 else jnp.logical_not(even)
        ref[s, x, :, z] = jnp.where(pick, high, low)


def first_sends(turns_x, turns_y, u_hbm, a_hbm, c_hbm, *refs):
    ys, refs = refs[:turns_y], refs[turns_y:]
    xs, refs = refs[:turns_x], refs[turns_x:]
    u_low, u_high, a_low, a_high, c_low, c_high, u_x, a_x, c_x, sems = refs
    shots, width_x, width_y, depth = u_hbm.shape
    copies = []

    def fetch(src, dst):
        copy = pltpu.make_async_copy(src, dst, sems.at[len(copies)])
        copy.start()
        copies.append(copy)

    for src, low, high in ((u_hbm, u_low, u_high), (a_hbm, a_low, a_high)):
        fetch(src.at[:, :, 0:8, :], low)
        fetch(src.at[:, :, width_y - 8 : width_y, :], high)
    fetch(c_hbm.at[:, 0:8, :], c_low)
    fetch(c_hbm.at[:, width_y - 8 : width_y, :], c_high)
    for turn in range(turns_x):
        first = jnp.minimum(
            edge_layer("gx", width_x, turn, 0), edge_layer("gx", width_x, turn, 3)
        )
        fetch(u_hbm.at[:, pl.ds(first, 4)], u_x.at[turn])
        fetch(a_hbm.at[:, pl.ds(first, 4)], a_x.at[turn])
        fetch(c_hbm.at[pl.ds(first, 4)], c_x.at[turn])
    for copy in copies:
        copy.wait()

    def line(x, carry):
        for z in halves(depth):
            mass_low = c_low[x, :, z] * c_low[x, :, z]
            mass_high = c_high[x, :, z] * c_high[x, :, z]
            for s in range(shots):
                write_y_sends(
                    ys,
                    s,
                    x,
                    z,
                    u_low[s, x, :, z],
                    mass_low * a_low[s, x, :, z],
                    u_high[s, x, :, z],
                    mass_high * a_high[s, x, :, z],
                )
        return carry

    lax.fori_loop(0, width_x, line, 0, unroll=4)
    for turn in range(turns_x):
        top = edge_layer("gx", width_x, turn, 0) > 3
        for k in range(4):
            layer = jnp.where(top, 3 - k, k)
            mass = c_x[turn, layer] * c_x[turn, layer]
            for s in range(shots):
                xs[turn][0, s, k] = u_x[turn, s, layer]
                xs[turn][1, s, k] = mass * a_x[turn, s, layer]


def depth_band(depth):
    apart = jnp.abs(
        lax.broadcasted_iota(jnp.int32, (depth, depth), 0)
        - lax.broadcasted_iota(jnp.int32, (depth, depth), 1)
    )
    band = jnp.zeros((depth, depth), F32)
    for r in range(1, 5):
        band = jnp.where(apart == r, float(round(5040 * COEFS[r])), band)
    return band.astype(BF16)


def three_parts(v):
    top = v.astype(BF16)
    rest = v - top.astype(F32)
    middle = rest.astype(BF16)
    return top, middle, (rest - middle.astype(F32)).astype(BF16)


def laplace_tile(field, deep, s, x, row):
    totals, centers = [], []
    for h in range(2):
        center = field[s, h, x + 4, pl.ds(row, 8), :]
        total = 3.0 * COEFS[0] * center + deep[:, h * 128 : h * 128 + 128]
        for r in range(1, 5):
            part = field[s, h, x + 4 + r, pl.ds(row, 8), :] + field[s, h, x + 4 - r, pl.ds(row, 8), :]
            part = part + field[s, h, x + 4, pl.ds(row + r, 8), :] + field[s, h, x + 4, pl.ds(row - r, 8), :]
            total = total + COEFS[r] * part
        centers.append(center)
        totals.append(total)
    return centers, totals


def march(offset, rows_y, step_ref, src_ref, wave_ref, rec_hbm, trace_hbm, u, u_old, a, a_old, cour, *refs):
    image_in, refs = (refs[0], refs[1:]) if offset else (None, refs)
    u_out, a_out, image, *refs = refs
    priors, refs = (refs[:2], refs[2:]) if offset else ((), refs)
    field_u, field_m, split, band, deep, trace, rec_ref, *olds, sems = refs
    shots, width_x, width_y, depth = u.shape
    tiles = width_y // 8
    copies = []

    def move(src, dst):
        copy = pltpu.make_async_copy(src, dst, sems.at[len(copies)])
        copy.start()
        copies.append(copy)
        return copy

    loads = [move(src, dst) for src, dst in zip((u_old, a_old), olds)]
    saves = [move(src, dst) for src, dst in zip((u, a), priors)]
    late = [move(rec_hbm, rec_ref)]
    u_old, a_old = olds or (u_old, a_old)
    for s in range(shots):
        moment = step_ref[s] - offset
        block = pl.multiple_of((moment // 8) * 8, 8)
        late.append(move(trace_hbm.at[s, pl.ds(block, 8), :], trace.at[s]))
    zero = jnp.zeros((8, 128), F32)
    for field in (field_u, field_m):
        for s in range(shots):
            for h in range(2):
                for x in (0, 1, 2, 3, width_x + 4, width_x + 5, width_x + 6, width_x + 7):
                    for t in range(1, tiles + 1):
                        field[s, h, x, 8 * t : 8 * t + 8, :] = zero

    for part in range(3):
        band[part * depth : part * depth + depth, :] = depth_band(depth)

    def fill(pair, carry):
        for k in range(2):
            x = 2 * pair + k
            mass = cour[x] * cour[x]
            for f, field in enumerate((field_u, field_m)):
                for s in range(shots):
                    block = mass * a[s, x] if f else u[s, x]
                    rows = ((k * 2 + f) * shots + s) * width_y
                    for part, value in enumerate(three_parts(block)):
                        split[rows : rows + width_y, part * depth : part * depth + depth] = value
                    for h, z in enumerate(halves(depth)):
                        field[s, h, x + 4, 0:8, :] = zero
                        field[s, h, x + 4, 8 : width_y + 8, :] = block[:, z]
                        field[s, h, x + 4, width_y + 8 : width_y + 16, :] = zero
        deep[pair] = jnp.dot(split[...], band[...], preferred_element_type=F32) * (1.0 / 5040.0)
        return carry

    lax.fori_loop(0, width_x // 2, fill, 0)
    for load in loads:
        load.wait()

    def line(x, carry):
        pair, side = x // 2, x % 2
        for t in range(tiles):
            row = slice(8 * t, 8 * t + 8)
            mass = [cour[x, row, z] * cour[x, row, z] for z in halves(depth)]
            terms = [image_in[h, x, row, :] if offset else None for h in range(2)]
            for s in range(shots):
                laps = []
                for f, field in enumerate((field_u, field_m)):
                    at = pl.multiple_of(((side * 2 + f) * shots + s) * width_y + 8 * t, 8)
                    laps.append(laplace_tile(field, deep[pair, pl.ds(at, 8), :], s, x, 8 * t + 8))
                (center, lap_u), (_, lap_a) = laps
                for h, z in enumerate(halves(depth)):
                    a_now = a[s, x, row, z]
                    term = a_now * lap_u[h]
                    terms[h] = term if terms[h] is None else terms[h] + term
                    u_out[s, x, row, z] = 2.0 * center[h] - u_old[s, x, row, z] + mass[h] * lap_u[h]
                    a_out[s, x, row, z] = 2.0 * a_now - a_old[s, x, row, z] + lap_a[h]
            for h in range(2):
                image[h, x, row, :] = terms[h]
        return carry

    lax.fori_loop(0, width_x, line, 0)

    for copy in late:
        copy.wait()
    bits = rows_y.bit_length() - 1
    anchor_x = lax.axis_index("gx") * width_x
    anchor_y = lax.axis_index("gy") * width_y
    lane, sub = iota(1), iota(0)
    for s in range(shots):
        moment = step_ref[s] - offset
        place_x = lax.shift_right_logical(src_ref[s], bits) - anchor_x
        place_y = (src_ref[s] & (rows_y - 1)) - anchor_y
        here = (place_x >= 0) & (place_x < width_x) & (place_y >= 0) & (place_y < width_y)

        @pl.when(here)
        def _():
            row = pl.ds(pl.multiple_of((place_y // 8) * 8, 8), 8)
            speed = cour[place_x, row, 0:128]
            hit = (sub == place_y % 8) & (lane == SRC_DEPTH)
            added = jnp.where(hit, speed * speed * wave_ref[s, moment], 0.0)
            u_out[s, place_x, row, 0:128] = u_out[s, place_x, row, 0:128] + added

        pick = lax.broadcasted_iota(jnp.int32, trace.shape[1:], 0) == moment % 8
        values = jnp.sum(jnp.where(pick, trace[s], 0.0), axis=0, keepdims=True)
        cells = rec_ref[s : s + 1, :]
        count = cells.shape[1]
        cell_x = lax.shift_right_logical(cells, bits) - anchor_x
        cell_y = (cells & (rows_y - 1)) - anchor_y
        hot_x = lax.broadcasted_iota(jnp.int32, (width_x, count), 0) == cell_x
        hot_y = lax.broadcasted_iota(jnp.int32, (width_y, count), 0) == cell_y
        spread = [jnp.where(hot_y, part.astype(F32), 0.0).astype(BF16) for part in three_parts(values)]
        planes = lax.dot_general(
            jnp.concatenate(spread, axis=0),
            jnp.where(hot_x, 1.0, 0.0).astype(BF16),
            (((1,), (1,)), ((), ())),
            preferred_element_type=F32,
        )
        plane = planes[0:width_y] + planes[width_y : 2 * width_y] + planes[2 * width_y :]
        depth_mask = lax.broadcasted_iota(jnp.int32, (width_y, 128), 1) == REC_DEPTH
        for x in range(width_x):
            added = jnp.where(depth_mask, plane[:, x : x + 1], 0.0)
            a_out[s, x, :, 0:128] = a_out[s, x, :, 0:128] + added
    for save in saves:
        save.wait()


def packed(load, target, x):
    lane = lax.broadcasted_iota(jnp.int32, (16, 128), 1)
    block = load(target // 2, x)
    top, bottom = block[0:16, :], block[16:32, :]
    front = jnp.where(lane < 64, top, pltpu.roll(bottom, 64, 1))
    back = jnp.where(lane < 64, pltpu.roll(top, 64, 1), bottom)
    return jnp.where(target % 2 == 0, front, back)


def edge(turns_x, turns_y, last, *refs):
    hy, refs = refs[:turns_y], refs[turns_y:]
    hx, refs = refs[:turns_x], refs[turns_x:]
    a, cour, _, _, _, u_out, a_out, image, *sends = refs
    shots, width_x, width_y, depth = a.shape
    sub = iota(0)
    even = even_on("gy")

    has_below, has_above = has_neighbour("gy", -1), has_neighbour("gy", 1)

    def coef(values):
        out = jnp.zeros((8, 128), F32)
        for j, v in values:
            out = jnp.where(sub == j, v, out)
        return out

    low_coef = [None] + [coef([(j, COEFS[r]) for j in range(4) if j < r]) for r in range(1, 5)]
    high_coef = [None] + [coef([(p, COEFS[r]) for p in range(4, 8) if p >= 8 - r]) for r in range(1, 5)]

    def turned(v, shift):
        return v if shift % 8 == 0 else pltpu.roll(v, shift % 8, 0)

    def rows(x, carry):
        for h, z in enumerate(halves(depth)):
            terms = [image[h, x, 0:8, :], image[h, x, width_y - 8 : width_y, :]]
            for s in range(shots):
                first = hy[0][s, x, :, z]
                second = hy[1][s, x, :, z] if turns_y > 1 else jnp.zeros_like(first)
                below = jnp.where(has_below, jnp.where(even, second, first), 0.0)
                above = jnp.where(has_above, jnp.where(even, first, second), 0.0)
                for side in range(2):
                    row = slice(0, 8) if side == 0 else slice(width_y - 8, width_y)
                    lap_u = lap_a = None
                    for r in range(1, 5):
                        if side == 0:
                            part_u = low_coef[r] * turned(below, r - 4)
                            part_a = low_coef[r] * turned(below, r)
                        else:
                            part_u = high_coef[r] * turned(above, 8 - r)
                            part_a = high_coef[r] * turned(above, 4 - r)
                        lap_u = part_u if lap_u is None else lap_u + part_u
                        lap_a = part_a if lap_a is None else lap_a + part_a
                    mass = cour[x, row, z] * cour[x, row, z]
                    u_out[s, x, row, z] = u_out[s, x, row, z] + mass * lap_u
                    a_out[s, x, row, z] = a_out[s, x, row, z] + lap_a
                    terms[side] = terms[side] + a[s, x, row, z] * lap_u
            image[h, x, 0:8, :] = terms[0]
            image[h, x, width_y - 8 : width_y, :] = terms[1]
        return carry

    lax.fori_loop(0, width_x, rows, 0, unroll=2)
    for turn in range(turns_x):
        toward = jnp.where(even_on("gx"), 1, -1) * (1 if turn == 0 else -1)
        whole = turn == 0 and lax.axis_size("gx") % 2 == 0
        for j in range(4):
            x = edge_layer("gx", width_x, turn, j)
            for h, z in enumerate(halves(depth)):
                term = image[h, x]
                for s in range(shots):
                    lap_u = lap_a = None
                    for k in range(4 - j):
                        part_u = COEFS[j + k + 1] * hx[turn][0, s, k, :, z]
                        part_a = COEFS[j + k + 1] * hx[turn][1, s, k, :, z]
                        lap_u = part_u if lap_u is None else lap_u + part_u
                        lap_a = part_a if lap_a is None else lap_a + part_a
                    if not whole:
                        lap_u = jnp.where(has_neighbour("gx", toward), lap_u, 0.0)
                        lap_a = jnp.where(has_neighbour("gx", toward), lap_a, 0.0)
                    mass = cour[x, :, z] * cour[x, :, z]
                    u_out[s, x, :, z] = u_out[s, x, :, z] + mass * lap_u
                    a_out[s, x, :, z] = a_out[s, x, :, z] + lap_a
                    term = term + a[s, x, :, z] * lap_u
                image[h, x] = term
    if last:
        me = lax.axis_index("shot")

        def parts(x, carry):
            for k, ref in enumerate(sends):
                ref[x] = packed(lambda h, x: image[h, x], me ^ k, x)
            return carry

        lax.fori_loop(0, width_x, parts, 0, unroll=2)
        return
    ys, xs = sends[:turns_y], sends[turns_y:]

    def outgoing(x, carry):
        for z in halves(depth):
            tile = []
            for row in (slice(0, 8), slice(width_y - 8, width_y)):
                mass = cour[x, row, z] * cour[x, row, z]
                tile.append((row, mass))
            for s in range(shots):
                (low, mass_low), (high, mass_high) = tile
                write_y_sends(
                    ys,
                    s,
                    x,
                    z,
                    u_out[s, x, low, z],
                    mass_low * a_out[s, x, low, z],
                    u_out[s, x, high, z],
                    mass_high * a_out[s, x, high, z],
                )
        return carry

    lax.fori_loop(0, width_x, outgoing, 0, unroll=4)
    for turn in range(turns_x):
        for k in range(4):
            x = edge_layer("gx", width_x, turn, k)
            mass = cour[x] * cour[x]
            for s in range(shots):
                xs[turn][0, s, k] = u_out[s, x]
                xs[turn][1, s, k] = mass * a_out[s, x]


def flush(u, a, u_out, a_out, sems):
    copies = [
        pltpu.make_async_copy(u, u_out, sems.at[0]),
        pltpu.make_async_copy(a, a_out, sems.at[1]),
    ]
    for copy in copies:
        copy.start()
    for copy in copies:
        copy.wait()


def finish(scale, cour, own, first, second, third, out):
    me = lax.axis_index("shot")

    def line(x, carry):
        speed = packed(lambda h, x: jnp.where(h == 0, cour[x, :, 0:128], cour[x, :, 128:256]), me, x)
        total = own[x] + first[x] + second[x] + third[x]
        value = 2.0 * speed * total / scale
        out[x, 0:16, :] = value[:, 0:64]
        out[x, 16:32, :] = value[:, 64:128]
        return carry

    lax.fori_loop(0, out.shape[0], line, 0, unroll=4)


def call(body, name, outs, scratch, in_specs, args, cost, aliases=None, out_specs=None, limit=24 << 20):
    return pl.pallas_call(
        body,
        name=name,
        out_shape=outs,
        in_specs=in_specs,
        out_specs=out_specs or [VMEM] * len(outs),
        scratch_shapes=scratch,
        input_output_aliases=aliases or {},
        compiler_params=pltpu.CompilerParams(vmem_limit_bytes=limit),
        cost_estimate=pl.CostEstimate(flops=cost, bytes_accessed=cost, transcendentals=0),
    )(*args)


def shards(
    fwd_now, fwd_next, adj_now, adj_next, courant, wavelet, traces, src_cells, rec_cells, step_index
):
    shots, width_x, width_y, depth = fwd_now.shape
    groups = lax.axis_size("shot")
    rows_y = width_y * lax.axis_size("gy")
    assert rows_y & (rows_y - 1) == 0 and depth == 256 and groups == 4 and width_y == 32
    perms_x, perms_y = pair_permutes("gx", "gy"), pair_permutes("gy", "gx")
    turns_x, turns_y = len(perms_x), len(perms_y)

    def shape(*dims):
        return jax.ShapeDtypeStruct(dims, F32)

    y_send, x_send = (shots, width_x, 8, depth), (2, shots, 4, width_y, depth)
    send_shapes = [shape(*y_send)] * turns_y + [shape(*x_send)] * turns_x
    y_rows, x_rows = (shots, width_x, 8, depth), (turns_x, shots, 4, width_y, depth)
    scratch = [pltpu.VMEM(y_rows, F32)] * 4 + [pltpu.VMEM(y_rows[1:], F32)] * 2
    scratch += [pltpu.VMEM(x_rows, F32)] * 2 + [pltpu.VMEM((turns_x, 4, width_y, depth), F32)]
    scratch += [pltpu.SemaphoreType.DMA((6 + 3 * turns_x,))]
    sends = call(
        functools.partial(first_sends, turns_x, turns_y),
        "first_sends",
        send_shapes,
        scratch,
        [HBM] * 3,
        (in_hbm(fwd_now), in_hbm(adj_now), in_hbm(courant)),
        1 << 20,
    )
    u_now, u_next, a_now, a_next = fwd_now, fwd_next, adj_now, adj_next
    image = None
    for offset in range(STEPS):
        last = offset == STEPS - 1
        halo_y = [lax.ppermute(s, ("gx", "gy"), p) for s, p in zip(sends[:turns_y], perms_y)]
        halo_x = [lax.ppermute(s, ("gx", "gy"), p) for s, p in zip(sends[turns_y:], perms_x)]
        padded = pltpu.VMEM((shots, 2, width_x + 8, width_y + 16, 128), F32)
        old = (u_next, a_next) if offset else (in_hbm(u_next), in_hbm(a_next))
        args = (step_index, src_cells, wavelet, in_hbm(rec_cells), in_hbm(traces))
        args += (u_now, old[0], a_now, old[1], courant)
        args += (image,) if offset else ()
        state = [shape(*fwd_now.shape)] * 2 + [shape(2, width_x, width_y, 128)]
        priors = [shape(*fwd_now.shape)] * 2 if offset else []
        u_prev, a_prev, image, *priors = call(
            functools.partial(march, offset, rows_y),
            f"march_{offset}",
            state + priors,
            [
                padded,
                padded,
                pltpu.VMEM((4 * shots * width_y, 3 * depth), BF16),
                pltpu.VMEM((3 * depth, depth), BF16),
                pltpu.VMEM((width_x // 2, 4 * shots * width_y, depth), F32),
                pltpu.VMEM((shots, 8, traces.shape[-1]), F32),
                pltpu.VMEM(rec_cells.shape, jnp.int32),
                *([] if offset else [pltpu.VMEM(fwd_now.shape, F32)] * 2),
                pltpu.SemaphoreType.DMA((shots + 3,)),
            ],
            [SMEM] * 3
            + [HBM] * 2
            + ([VMEM] * 4 if offset else [VMEM, HBM] * 2)
            + [VMEM] * (len(args) - 9),
            args,
            16 << 20,
            out_specs=[VMEM] * 3 + [HBM] * len(priors),
        )
        args = (*halo_y, *halo_x, a_now, courant, in_vmem(u_prev), in_vmem(a_prev), in_vmem(image))
        base = len(args) - 3
        outs = state + ([shape(width_x, 16, 128)] * groups if last else send_shapes)
        u_prev, a_prev, image, *sends = call(
            functools.partial(edge, turns_x, turns_y, last),
            f"edge_{offset}",
            outs,
            [],
            [VMEM] * len(args),
            args,
            2 << 20,
            {base: 0, base + 1: 1, base + 2: 2},
        )
        u_next, u_now = u_now, u_prev
        a_next, a_now = a_now, a_prev
    starts = call(
        flush,
        "flush",
        [shape(*fwd_now.shape)] * 2,
        [pltpu.SemaphoreType.DMA((2,))],
        [VMEM] * 2,
        (in_vmem(u_now), in_vmem(a_now)),
        4 << 20,
        out_specs=[HBM] * 2,
    )
    parts = [sends[0]]
    for k in range(1, groups):
        parts.append(lax.ppermute(sends[k], "shot", [(i, i ^ k) for i in range(groups)]))
    (gradient,) = call(
        functools.partial(finish, float(shots * groups * STEPS)),
        "finish",
        [shape(width_x, width_y, depth // groups)],
        [],
        [VMEM] * 5,
        (courant, *parts),
        1 << 20,
    )
    return (priors[0], starts[0], priors[1], starts[1], gradient)


def solution(mesh):
    fields = P("shot", "gx", "gy", None)
    in_specs = (fields,) * 4 + (
        P("gx", "gy", None),
        P("shot", None),
        P("shot", None, None),
        P("shot"),
        P("shot", None),
        P("shot"),
    )
    out_specs = (fields,) * 4 + (P("gx", "gy", "shot"),)
    return jax.shard_map(shards, mesh=mesh, in_specs=in_specs, out_specs=out_specs, check_vma=False)
```

```python
import functools

import jax
import jax.numpy as jnp
from jax import lax
from jax.experimental import pallas as pl
from jax.experimental.pallas import tpu as pltpu
from jax.sharding import PartitionSpec as P

STEPS = 2
SRC_DEPTH = 4
REC_DEPTH = 6
COEFS = (-205.0 / 72.0, 8.0 / 5.0, -1.0 / 5.0, 8.0 / 315.0, -1.0 / 560.0)
F32 = jnp.float32
BF16 = jnp.bfloat16
VMEM = pl.BlockSpec(memory_space=pltpu.VMEM)
SMEM = pl.BlockSpec(memory_space=pltpu.SMEM)
HBM = pl.BlockSpec(memory_space=pltpu.HBM)


def iota(dim):
    return lax.broadcasted_iota(jnp.int32, (8, 128), dim)


def even_on(axis):
    return lax.axis_index(axis) % 2 == 0


def pair_permutes(axis, other):
    count, across = lax.axis_size(axis), lax.axis_size(other)
    perms = []

    def at(i, j):
        return i * across + j if axis == "gx" else j * count + i

    for first in (0, 1):
        pairs = [(i, i + 1) for i in range(first, count - 1, 2)]
        if not pairs:
            continue
        left = set(range(count)) - {i for pair in pairs for i in pair}
        perm = [(at(a, j), at(b, j)) for a, b in pairs for j in range(across)]
        perm += [(b, a) for a, b in perm]
        if across % 2 == 0:
            perm += [(at(i, j), at(i, j ^ 1)) for i in sorted(left) for j in range(across)]
        perms.append(perm)
    return perms


def has_neighbour(axis, step):
    at = lax.axis_index(axis) + step
    return (at >= 0) & (at < lax.axis_size(axis))


def edge_layer(axis, width, turn, k):
    high = even_on(axis) if turn == 0 else jnp.logical_not(even_on(axis))
    return jnp.where(high, width - 1 - k, k)


def in_hbm(x):
    return pltpu.with_memory_space_constraint(x, pltpu.HBM)


def in_vmem(x):
    return pltpu.with_memory_space_constraint(x, pltpu.VMEM)


def halves(depth):
    return [slice(h * 128, h * 128 + 128) for h in range(depth // 128)]


def write_y_sends(sends, at, x, z, low_0, low_1, high_0, high_1):
    sub = iota(0)
    low = jnp.where(sub < 4, low_0, pltpu.roll(low_1, 4, 0))
    high = jnp.where(sub < 4, pltpu.roll(high_0, 4, 0), high_1)
    even = even_on("gy")
    for turn, ref in enumerate(sends):
        pick = even if turn == 0 else jnp.logical_not(even)
        ref[at, x, :, z] = jnp.where(pick, high, low)


def first_sends(turns_x, turns_y, u_hbm, a_hbm, c_hbm, *refs):
    ys, refs = refs[:turns_y], refs[turns_y:]
    xs, refs = refs[:turns_x], refs[turns_x:]
    u_low, u_high, a_low, a_high, c_low, c_high, u_x, a_x, c_x, sems = refs
    shots, width_x, width_y, depth = u_hbm.shape
    copies = []

    def fetch(src, dst):
        copy = pltpu.make_async_copy(src, dst, sems.at[len(copies)])
        copy.start()
        copies.append(copy)

    for src, low, high in ((u_hbm, u_low, u_high), (a_hbm, a_low, a_high)):
        fetch(src.at[:, :, 0:8, :], low)
        fetch(src.at[:, :, width_y - 8 : width_y, :], high)
    fetch(c_hbm.at[:, 0:8, :], c_low)
    fetch(c_hbm.at[:, width_y - 8 : width_y, :], c_high)
    for turn in range(turns_x):
        first = jnp.minimum(
            edge_layer("gx", width_x, turn, 0), edge_layer("gx", width_x, turn, 3)
        )
        fetch(u_hbm.at[:, pl.ds(first, 4)], u_x.at[turn])
        fetch(a_hbm.at[:, pl.ds(first, 4)], a_x.at[turn])
        fetch(c_hbm.at[pl.ds(first, 4)], c_x.at[turn])
    for copy in copies:
        copy.wait()

    def line(x, carry):
        for z in halves(depth):
            low = c_low[x, :, z] * c_low[x, :, z]
            high = c_high[x, :, z] * c_high[x, :, z]
            write_y_sends(ys, 0, x, z, *(ref[s, x, :, z] for ref in (u_low, u_high) for s in range(2)))
            write_y_sends(
                ys,
                1,
                x,
                z,
                *(m * ref[s, x, :, z] for m, ref in ((low, a_low), (high, a_high)) for s in range(2)),
            )
        return carry

    lax.fori_loop(0, width_x, line, 0, unroll=4)
    for turn in range(turns_x):
        top = edge_layer("gx", width_x, turn, 0) > 3
        for k in range(4):
            layer = jnp.where(top, 3 - k, k)
            mass = c_x[turn, layer] * c_x[turn, layer]
            for s in range(shots):
                xs[turn][0, s, k] = u_x[turn, s, layer]
                xs[turn][1, s, k] = mass * a_x[turn, s, layer]


def band_of(apart):
    band = jnp.zeros(apart.shape, F32)
    for r in range(1, 5):
        band = jnp.where(apart == r, float(round(5040 * COEFS[r])), band)
    return band.astype(BF16)


def make_bands(band_y, band_z):
    rows, columns = band_y.shape
    at = lax.broadcasted_iota(jnp.int32, (rows, columns), 1) % rows
    band_y[...] = band_of(jnp.abs(at - lax.broadcasted_iota(jnp.int32, (rows, columns), 0)))
    depth = band_z.shape[1]
    at = lax.broadcasted_iota(jnp.int32, (depth, depth), 0)
    band = band_of(jnp.abs(at - lax.broadcasted_iota(jnp.int32, (depth, depth), 1)))
    for part in range(3):
        band_z[part * depth : part * depth + depth, :] = band


def three_parts(v):
    top = v.astype(BF16)
    rest = v - top.astype(F32)
    middle = rest.astype(BF16)
    return top, middle, (rest - middle.astype(F32)).astype(BF16)


BATCH = 4


def plane_stencil(block_of, shots, band_y, band_z, split, flat):
    depth = band_z.shape[1]
    width_y = band_y.shape[0]

    def layers(batch, carry):
        along_y = []
        for k in range(BATCH):
            for s in range(shots):
                parts = three_parts(block_of(s, BATCH * batch + k))
                rows = (k * shots + s) * width_y
                for part, value in enumerate(parts):
                    split[rows : rows + width_y, part * depth : part * depth + depth] = value
                stacked = jnp.concatenate(parts, axis=0)
                along_y.append(jnp.dot(band_y[...], stacked, preferred_element_type=F32))
        along_z = jnp.dot(split[...], band_z[...], preferred_element_type=F32)
        for k in range(BATCH):
            for s in range(shots):
                rows = (k * shots + s) * width_y
                both = along_z[rows : rows + width_y, :] + along_y[k * shots + s]
                flat[s, BATCH * batch + k] = both * (1.0 / 5040.0)
        return carry

    lax.fori_loop(0, flat.shape[1] // BATCH, layers, 0)


def laplace_line(field, flat, s, row, z):
    width_x = flat.shape[1]
    line = [field[s, x, row, z] for x in range(width_x)]
    for x in range(width_x):
        total = 3.0 * COEFS[0] * line[x] + flat[s, x, row, z]
        for r in range(1, 5):
            near = [line[i] for i in (x - r, x + r) if 0 <= i < width_x]
            if near:
                total = total + COEFS[r] * (near[0] if len(near) == 1 else near[0] + near[1])
        yield x, line[x], total


class Copies:
    def __init__(self, sems):
        self.sems, self.count = sems, 0

    def start(self, src, dst):
        copy = pltpu.make_async_copy(src, dst, self.sems.at[self.count])
        copy.start()
        self.count += 1
        return copy


def place(cells, rows_y, width_x, width_y):
    bits = rows_y.bit_length() - 1
    x = lax.shift_right_logical(cells, bits) - lax.axis_index("gx") * width_x
    y = (cells & (rows_y - 1)) - lax.axis_index("gy") * width_y
    return x, y


def forward_march(offset, rows_y, step_ref, src_ref, wave_ref, u, u_old, a, cour, *refs):
    if offset:
        band_y, band_z, image_in, u_out, image, prior, *refs = refs
    else:
        u_out, image, band_y, band_z, *refs = refs
    split, flat, *old, sems = refs
    shots, width_x, width_y, depth = u.shape
    copies = Copies(sems)
    moves = [copies.start(u, prior) if offset else copies.start(u_old, old[0])]
    u_old = u_old if offset else old[0]
    if not offset:
        make_bands(band_y, band_z)
    plane_stencil(lambda s, x: u[s, x], shots, band_y, band_z, split, flat)
    if not offset:
        moves.pop().wait()

    def tiles(t, carry):
        row = pl.ds(pl.multiple_of(8 * t, 8), 8)
        for h, z in enumerate(halves(depth)):
            for s in range(shots):
                for x, center, lap in laplace_line(u, flat, s, row, z):
                    mass = cour[x, row, z] * cour[x, row, z]
                    u_out[s, x, row, z] = 2.0 * center - u_old[s, x, row, z] + mass * lap
                    term = a[s, x, row, z] * lap
                    if s:
                        image[h, x, row, :] = image[h, x, row, :] + term
                    else:
                        image[h, x, row, :] = image_in[h, x, row, :] + term if offset else term
        return carry

    lax.fori_loop(0, width_y // 8, tiles, 0)
    lane, sub = iota(1), iota(0)
    for s in range(shots):
        at_x, at_y = place(src_ref[s], rows_y, width_x, width_y)

        @pl.when((at_x >= 0) & (at_x < width_x) & (at_y >= 0) & (at_y < width_y))
        def _():
            row = pl.ds(pl.multiple_of((at_y // 8) * 8, 8), 8)
            speed = cour[at_x, row, 0:128]
            hit = (sub == at_y % 8) & (lane == SRC_DEPTH)
            added = jnp.where(hit, speed * speed * wave_ref[s, step_ref[s] - offset], 0.0)
            u_out[s, at_x, row, 0:128] = u_out[s, at_x, row, 0:128] + added

    for move in moves:
        move.wait()


def adjoint_march(offset, rows_y, step_ref, rec_hbm, trace_hbm, a, a_old, cour, band_y, band_z, *refs):
    done, refs = (refs[0], refs[1:]) if offset else (None, refs)
    a_out, *refs = refs
    outs, refs = (refs[:2], refs[2:]) if offset else ((), refs)
    split, flat, scaled, trace, rec_ref, *old, sems = refs
    shots, width_x, width_y, depth = a.shape
    copies = Copies(sems)
    loads = [copies.start(rec_hbm, rec_ref)]
    for s in range(shots):
        block = pl.multiple_of(((step_ref[s] - offset) // 8) * 8, 8)
        loads.append(copies.start(trace_hbm.at[s, pl.ds(block, 8), :], trace.at[s]))
    if offset:
        moves = [copies.start(src, dst) for src, dst in zip((a, done), outs)]
    else:
        moves = [copies.start(a_old, old[0])]
        a_old = old[0]

    def scale(s, x):
        block = cour[x] * cour[x] * a[s, x]
        scaled[s, x] = block
        return block

    plane_stencil(scale, shots, band_y, band_z, split, flat)
    if not offset:
        moves.pop().wait()

    def tiles(t, carry):
        row = pl.ds(pl.multiple_of(8 * t, 8), 8)
        for z in halves(depth):
            for s in range(shots):
                for x, _, lap in laplace_line(scaled, flat, s, row, z):
                    a_out[s, x, row, z] = 2.0 * a[s, x, row, z] - a_old[s, x, row, z] + lap
        return carry

    lax.fori_loop(0, width_y // 8, tiles, 0)
    for load in loads:
        load.wait()
    for s in range(shots):
        moment = step_ref[s] - offset
        pick = lax.broadcasted_iota(jnp.int32, trace.shape[1:], 0) == moment % 8
        values = jnp.sum(jnp.where(pick, trace[s], 0.0), axis=0, keepdims=True)
        at_x, at_y = place(rec_ref[s : s + 1, :], rows_y, width_x, width_y)
        count = at_x.shape[1]
        hot_x = lax.broadcasted_iota(jnp.int32, (width_x, count), 0) == at_x
        hot_y = lax.broadcasted_iota(jnp.int32, (width_y, count), 0) == at_y
        spread = [jnp.where(hot_y, part.astype(F32), 0.0).astype(BF16) for part in three_parts(values)]
        planes = lax.dot_general(
            jnp.concatenate(spread, axis=0),
            jnp.where(hot_x, 1.0, 0.0).astype(BF16),
            (((1,), (1,)), ((), ())),
            preferred_element_type=F32,
        )
        plane = planes[0:width_y] + planes[width_y : 2 * width_y] + planes[2 * width_y :]
        depth_mask = lax.broadcasted_iota(jnp.int32, (width_y, 128), 1) == REC_DEPTH
        for x in range(width_x):
            added = jnp.where(depth_mask, plane[:, x : x + 1], 0.0)
            a_out[s, x, :, 0:128] = a_out[s, x, :, 0:128] + added
    for move in moves:
        move.wait()


def packed(load, target, x):
    lane = lax.broadcasted_iota(jnp.int32, (16, 128), 1)
    block = load(target // 2, x)
    top, bottom = block[0:16, :], block[16:32, :]
    front = jnp.where(lane < 64, top, pltpu.roll(bottom, 64, 1))
    back = jnp.where(lane < 64, pltpu.roll(top, 64, 1), bottom)
    return jnp.where(target % 2 == 0, front, back)


def add_edges(hy, hx, field_at, out, cour, forward, a, image):
    shots, width_x, width_y, depth = out.shape
    sub = iota(0)
    even = even_on("gy")
    has_below, has_above = has_neighbour("gy", -1), has_neighbour("gy", 1)

    def coef(values):
        row = jnp.zeros((8, 128), F32)
        for j, v in values:
            row = jnp.where(sub == j, v, row)
        return row

    low_coef = [None] + [coef([(j, COEFS[r]) for j in range(4) if j < r]) for r in range(1, 5)]
    high_coef = [None] + [coef([(p, COEFS[r]) for p in range(4, 8) if p >= 8 - r]) for r in range(1, 5)]

    def turned(v, shift):
        return v if shift % 8 == 0 else pltpu.roll(v, shift % 8, 0)

    def rows(x, carry):
        for h, z in enumerate(halves(depth)):
            first = hy[0][field_at, x, :, z]
            second = hy[1][field_at, x, :, z] if len(hy) > 1 else jnp.zeros_like(first)
            below = jnp.where(has_below, jnp.where(even, second, first), 0.0)
            above = jnp.where(has_above, jnp.where(even, first, second), 0.0)
            for side in range(2):
                row = slice(0, 8) if side == 0 else slice(width_y - 8, width_y)
                for s in range(shots):
                    lap = None
                    for r in range(1, 5):
                        if side == 0:
                            part = low_coef[r] * turned(below, r - 4 + 4 * s)
                        else:
                            part = high_coef[r] * turned(above, 8 - r - 4 * s)
                        lap = part if lap is None else lap + part
                    if forward:
                        mass = cour[x, row, z] * cour[x, row, z]
                        out[s, x, row, z] = out[s, x, row, z] + mass * lap
                        image[h, x, row, :] = image[h, x, row, :] + a[s, x, row, z] * lap
                    else:
                        out[s, x, row, z] = out[s, x, row, z] + lap
        return carry

    lax.fori_loop(0, width_x, rows, 0, unroll=4)
    for turn, ref in enumerate(hx):
        toward = jnp.where(even_on("gx"), 1, -1) * (1 if turn == 0 else -1)
        whole = turn == 0 and lax.axis_size("gx") % 2 == 0
        for j in range(4):
            x = edge_layer("gx", width_x, turn, j)
            for h, z in enumerate(halves(depth)):
                for s in range(shots):
                    lap = None
                    for k in range(4 - j):
                        part = COEFS[j + k + 1] * ref[field_at, s, k, :, z]
                        lap = part if lap is None else lap + part
                    if not whole:
                        lap = jnp.where(has_neighbour("gx", toward), lap, 0.0)
                    if forward:
                        mass = cour[x, :, z] * cour[x, :, z]
                        out[s, x, :, z] = out[s, x, :, z] + mass * lap
                        image[h, x] = image[h, x] + a[s, x, :, z] * lap
                    else:
                        out[s, x, :, z] = out[s, x, :, z] + lap


def write_sends(turns_y, sends, out, cour):
    shots, width_x, width_y, depth = out.shape
    ys, xs = sends[:turns_y], sends[turns_y:]

    def line(x, carry):
        for z in halves(depth):
            tiles = []
            for row in (slice(0, 8), slice(width_y - 8, width_y)):
                for s in range(shots):
                    tile = out[s, x, row, z]
                    tiles.append(tile if cour is None else cour[x, row, z] * cour[x, row, z] * tile)
            write_y_sends(ys, 0, x, z, *tiles)
        return carry

    lax.fori_loop(0, width_x, line, 0, unroll=4)
    for turn, ref in enumerate(xs):
        for k in range(4):
            x = edge_layer("gx", width_x, turn, k)
            for s in range(shots):
                ref[0, s, k] = out[s, x] if cour is None else cour[x] * cour[x] * out[s, x]


def forward_edge(turns_x, turns_y, last, *refs):
    hy, hx, refs = refs[:turns_y], refs[turns_y : turns_y + turns_x], refs[turns_y + turns_x :]
    a, cour, *refs = refs
    u_out, image, *sends = refs[2 if last else 3 :]
    add_edges(hy, hx, 0, u_out, cour, True, a, image)
    if not last:
        write_sends(turns_y, sends, u_out, None)
        return
    me = lax.axis_index("shot")

    def parts(x, carry):
        for k, ref in enumerate(sends):
            ref[x] = packed(lambda h, x: image[h, x], me ^ k, x)
        return carry

    lax.fori_loop(0, u_out.shape[1], parts, 0, unroll=2)


def adjoint_edge(turns_x, turns_y, field_at, last, *refs):
    hy, hx, refs = refs[:turns_y], refs[turns_y : turns_y + turns_x], refs[turns_y + turns_x :]
    cour, _, a_out, *refs = refs
    add_edges(hy, hx, field_at, a_out, cour, False, None, None)
    if not last:
        write_sends(turns_y, refs, a_out, cour)
        return
    final, sem = refs
    copy = pltpu.make_async_copy(a_out, final, sem.at[0])
    copy.start()
    copy.wait()


def finish(scale, cour, own, first, second, third, out):
    me = lax.axis_index("shot")

    def line(x, carry):
        speed = packed(lambda h, x: jnp.where(h == 0, cour[x, :, 0:128], cour[x, :, 128:256]), me, x)
        total = own[x] + first[x] + second[x] + third[x]
        value = 2.0 * speed * total / scale
        out[x, 0:16, :] = value[:, 0:64]
        out[x, 16:32, :] = value[:, 64:128]
        return carry

    lax.fori_loop(0, out.shape[0], line, 0, unroll=4)


def call(body, name, outs, scratch, in_specs, args, cost, aliases=None, out_specs=None, limit=24 << 20):
    return pl.pallas_call(
        body,
        name=name,
        out_shape=outs,
        in_specs=in_specs,
        out_specs=out_specs or [VMEM] * len(outs),
        scratch_shapes=scratch,
        input_output_aliases=aliases or {},
        compiler_params=pltpu.CompilerParams(vmem_limit_bytes=limit),
        cost_estimate=pl.CostEstimate(flops=cost, bytes_accessed=cost, transcendentals=0),
    )(*args)


def shards(
    fwd_now, fwd_next, adj_now, adj_next, courant, wavelet, traces, src_cells, rec_cells, step_index
):
    shots, width_x, width_y, depth = fwd_now.shape
    groups = lax.axis_size("shot")
    rows_y = width_y * lax.axis_size("gy")
    assert rows_y & (rows_y - 1) == 0 and depth == 256 and groups == 4 and width_y == 32 and shots == 2
    perms_x, perms_y = pair_permutes("gx", "gy"), pair_permutes("gy", "gx")
    turns_x, turns_y = len(perms_x), len(perms_y)

    def shape(*dims):
        return jax.ShapeDtypeStruct(dims, F32)

    def swap_y(sends):
        return [lax.ppermute(s, ("gx", "gy"), p) for s, p in zip(sends, perms_y)]

    def swap_x(sends):
        return [lax.ppermute(s, ("gx", "gy"), p) for s, p in zip(sends, perms_x)]

    wave = shape(*fwd_now.shape)
    strip = shape(2, width_x, width_y, 128)
    y_send, x_rows = (width_x, 8, depth), (shots, 4, width_y, depth)
    y_rows = (shots, width_x, 8, depth)
    scratch = [pltpu.VMEM(y_rows, F32)] * 4 + [pltpu.VMEM(y_rows[1:], F32)] * 2
    scratch += [pltpu.VMEM((turns_x, *x_rows), F32)] * 2 + [pltpu.VMEM((turns_x, *x_rows[1:]), F32)]
    scratch += [pltpu.SemaphoreType.DMA((6 + 3 * turns_x,))]
    first = call(
        functools.partial(first_sends, turns_x, turns_y),
        "first_sends",
        [shape(2, *y_send)] * turns_y + [shape(2, *x_rows)] * turns_x,
        scratch,
        [HBM] * 3,
        (in_hbm(fwd_now), in_hbm(adj_now), in_hbm(courant)),
        1 << 20,
    )
    hx_u = hx_a = swap_x(first[turns_y:])
    hy_u = hy_a = swap_y(first[:turns_y])
    next_sends = [shape(1, *y_send)] * turns_y + [shape(1, *x_rows)] * turns_x
    bands = [jax.ShapeDtypeStruct((width_y, 3 * width_y), BF16), jax.ShapeDtypeStruct((3 * depth, depth), BF16)]
    stencil = [
        pltpu.VMEM((BATCH * shots * width_y, 3 * depth), BF16),
        pltpu.VMEM(fwd_now.shape, F32),
    ]
    sample = [pltpu.VMEM((shots, 8, traces.shape[-1]), F32), pltpu.VMEM(rec_cells.shape, jnp.int32)]
    u_now, u_next, a_now, a_next = fwd_now, fwd_next, adj_now, adj_next
    image = None
    for offset in range(STEPS):
        last = offset == STEPS - 1
        old_spec = VMEM if offset else HBM
        old_rows = [] if offset else [pltpu.VMEM(fwd_now.shape, F32)]
        old = u_next if offset else in_hbm(u_next)
        u_prev, image, *rest = call(
            functools.partial(forward_march, offset, rows_y),
            f"forward_march_{offset}",
            [wave, strip] + ([wave] if offset else bands),
            stencil + old_rows + [pltpu.SemaphoreType.DMA((1,))],
            [SMEM] * 3 + [VMEM, old_spec] + [VMEM] * (2 + 3 * offset),
            (step_index, src_cells, wavelet, u_now, old, a_now, courant) + ((*bands, image) if offset else ()),
            8 << 20,
            out_specs=[VMEM] * 2 + ([HBM] if offset else [VMEM] * 2),
        )
        if offset:
            forward_prior = rest[0]
        else:
            bands = rest
        def run_forward_edge(u_prev, image, *after):
            args = (*hy_u, *hx_u, a_now, courant, *after, in_vmem(u_prev), in_vmem(image))
            return call(
                functools.partial(forward_edge, turns_x, turns_y, last),
                f"forward_edge_{offset}",
                [wave, strip] + ([shape(width_x, 16, 128)] * groups if last else next_sends),
                [],
                [VMEM] * len(args),
                args,
                1 << 20,
                {len(args) - 2: 0, len(args) - 1: 1},
            )
        def run_adjoint_march(*done):
            old = a_next if offset else in_hbm(a_next)
            return call(
                functools.partial(adjoint_march, offset, rows_y),
                f"adjoint_march_{offset}",
                [wave] * (1 + 2 * offset),
                stencil + stencil[1:] + sample + old_rows + [pltpu.SemaphoreType.DMA((shots + 3,))],
                [SMEM] + [HBM] * 2 + [VMEM, old_spec] + [VMEM] * (3 + offset),
                (step_index, in_hbm(rec_cells), in_hbm(traces), a_now, old, courant, *bands)
                + tuple(in_vmem(d) for d in done),
                8 << 20,
                out_specs=[VMEM] + [HBM] * (2 * offset),
            )
        if offset:
            u_prev, image, *u_sends = run_forward_edge(u_prev, image)
            a_prev, *rest = run_adjoint_march(u_prev)
        else:
            a_prev, *rest = run_adjoint_march()
            u_prev, image, *u_sends = run_forward_edge(u_prev, image, a_prev)
        if last:
            parts = [u_sends[0]]
            for k in (3, 1, 2):
                parts.append(lax.ppermute(u_sends[k], "shot", [(i, i ^ k) for i in range(groups)]))
        else:
            hx_u, hy_u = swap_x(u_sends[turns_y:]), swap_y(u_sends[:turns_y])
        if offset:
            adjoint_prior, forward_start = rest
        args = (*hy_a, *hx_a, courant, in_vmem(a_prev))
        a_prev, *a_sends = call(
            functools.partial(adjoint_edge, turns_x, turns_y, 0 if offset else 1, last),
            f"adjoint_edge_{offset}",
            [wave] + ([wave] if last else next_sends),
            [pltpu.SemaphoreType.DMA((1,))] if last else [],
            [VMEM] * len(args),
            args,
            1 << 20,
            {len(args) - 1: 0},
            out_specs=[VMEM, HBM] if last else None,
        )
        if last:
            (adjoint_start,) = a_sends
        else:
            hx_a, hy_a = swap_x(a_sends[turns_y:]), swap_y(a_sends[:turns_y])
        u_next, u_now = u_now, u_prev
        a_next, a_now = a_now, a_prev
    (gradient,) = call(
        functools.partial(finish, float(shots * groups * STEPS)),
        "finish",
        [shape(width_x, width_y, depth // groups)],
        [],
        [VMEM] * 5,
        (courant, *parts),
        1 << 20,
    )
    return (forward_prior, forward_start, adjoint_prior, adjoint_start, gradient)


def solution(mesh):
    fields = P("shot", "gx", "gy", None)
    in_specs = (fields,) * 4 + (
        P("gx", "gy", None),
        P("shot", None),
        P("shot", None, None),
        P("shot"),
        P("shot", None),
        P("shot"),
    )
    out_specs = (fields,) * 4 + (P("gx", "gy", "shot"),)
    return jax.shard_map(shards, mesh=mesh, in_specs=in_specs, out_specs=out_specs, check_vma=False)
```

```python
import functools

import jax
import jax.numpy as jnp
from jax import lax
from jax.experimental import pallas as pl
from jax.experimental.pallas import tpu as pltpu
from jax.sharding import PartitionSpec as P


STEPS = 2
SRC_DEPTH = 4
REC_DEPTH = 6
COEFS = (-205.0 / 72.0, 8.0 / 5.0, -1.0 / 5.0, 8.0 / 315.0, -1.0 / 560.0)
F32 = jnp.float32
BF16 = jnp.bfloat16
VMEM = pl.BlockSpec(memory_space=pltpu.VMEM)
SMEM = pl.BlockSpec(memory_space=pltpu.SMEM)
HBM = pl.BlockSpec(memory_space=pltpu.HBM)


def iota(dim):
    return lax.broadcasted_iota(jnp.int32, (8, 128), dim)


def even_on(axis):
    return lax.axis_index(axis) % 2 == 0


def pair_permutes(axis, other):
    count, across = lax.axis_size(axis), lax.axis_size(other)
    perms = []

    def at(i, j):
        return i * across + j if axis == "gx" else j * count + i

    for first in (0, 1):
        pairs = [(i, i + 1) for i in range(first, count - 1, 2)]
        if not pairs:
            continue
        left = set(range(count)) - {i for pair in pairs for i in pair}
        perm = [(at(a, j), at(b, j)) for a, b in pairs for j in range(across)]
        perm += [(b, a) for a, b in perm]
        if across % 2 == 0:
            perm += [(at(i, j), at(i, j ^ 1)) for i in sorted(left) for j in range(across)]
        perms.append(perm)
    return perms


def has_neighbour(axis, step):
    at = lax.axis_index(axis) + step
    return (at >= 0) & (at < lax.axis_size(axis))


def edge_layer(axis, width, turn, k):
    high = even_on(axis) if turn == 0 else jnp.logical_not(even_on(axis))
    return jnp.where(high, width - 1 - k, k)


def in_hbm(x):
    return pltpu.with_memory_space_constraint(x, pltpu.HBM)


def in_vmem(x):
    return pltpu.with_memory_space_constraint(x, pltpu.VMEM)


def halves(depth):
    return [slice(h * 128, h * 128 + 128) for h in range(depth // 128)]


def write_y_sends(sends, at, x, z, low_0, low_1, high_0, high_1):
    sub = iota(0)
    low = jnp.where(sub < 4, low_0, pltpu.roll(low_1, 4, 0))
    high = jnp.where(sub < 4, pltpu.roll(high_0, 4, 0), high_1)
    even = even_on("gy")
    for turn, ref in enumerate(sends):
        pick = even if turn == 0 else jnp.logical_not(even)
        ref[at, x, :, z] = jnp.where(pick, high, low)


class Copies:
    def __init__(self, sems):
        self.sems, self.count = sems, 0

    def start(self, src, dst):
        copy = pltpu.make_async_copy(src, dst, self.sems.at[self.count])
        copy.start()
        self.count += 1
        return copy


def first_y_sends(u_hbm, a_hbm, c_hbm, *refs):
    *ys, u_low, u_high, a_low, a_high, c_low, c_high, sems = refs
    _, width_x, width_y, depth = u_hbm.shape
    copies = Copies(sems)
    waits = []
    for src, low, high in ((u_hbm, u_low, u_high), (a_hbm, a_low, a_high)):
        waits.append(copies.start(src.at[:, :, 0:8, :], low))
        waits.append(copies.start(src.at[:, :, width_y - 8 : width_y, :], high))
    waits.append(copies.start(c_hbm.at[:, 0:8, :], c_low))
    waits.append(copies.start(c_hbm.at[:, width_y - 8 : width_y, :], c_high))
    for wait in waits:
        wait.wait()

    def line(x, carry):
        for z in halves(depth):
            low = c_low[x, :, z] * c_low[x, :, z]
            high = c_high[x, :, z] * c_high[x, :, z]
            write_y_sends(ys, 0, x, z, *(ref[s, x, :, z] for ref in (u_low, u_high) for s in range(2)))
            write_y_sends(
                ys,
                1,
                x,
                z,
                *(m * ref[s, x, :, z] for m, ref in ((low, a_low), (high, a_high)) for s in range(2)),
            )
        return carry

    lax.fori_loop(0, width_x, line, 0, unroll=4)


def first_x_sends(u, a, cour, *xs):
    shots, width_x = u.shape[:2]
    for turn, ref in enumerate(xs):
        for k in range(4):
            x = edge_layer("gx", width_x, turn, k)
            for s in range(shots):
                ref[0, s, k] = u[s, x]
                ref[1, s, k] = cour[x] * cour[x] * a[s, x]


def band_of(apart):
    band = jnp.zeros(apart.shape, F32)
    for r in range(1, 5):
        band = jnp.where(apart == r, float(round(5040 * COEFS[r])), band)
    return band.astype(BF16)


def make_bands(band_y, band_z):
    rows, columns = band_y.shape
    at = lax.broadcasted_iota(jnp.int32, (rows, columns), 1) % rows
    band_y[...] = band_of(jnp.abs(at - lax.broadcasted_iota(jnp.int32, (rows, columns), 0)))
    depth = band_z.shape[1]
    at = lax.broadcasted_iota(jnp.int32, (depth, depth), 0)
    band = band_of(jnp.abs(at - lax.broadcasted_iota(jnp.int32, (depth, depth), 1)))
    for part in range(3):
        band_z[part * depth : part * depth + depth, :] = band


def three_parts(v):
    top = v.astype(BF16)
    rest = v - top.astype(F32)
    middle = rest.astype(BF16)
    return top, middle, (rest - middle.astype(F32)).astype(BF16)


BATCH = 8


def plane_stencil(block_of, shots, band_y, band_z, split, flat):
    depth = band_z.shape[1]
    width_y = band_y.shape[0]

    def layers(batch, carry):
        along_y = []
        for k in range(BATCH):
            for s in range(shots):
                parts = three_parts(block_of(s, BATCH * batch + k))
                rows = (k * shots + s) * width_y
                for part, value in enumerate(parts):
                    split[rows : rows + width_y, part * depth : part * depth + depth] = value
                stacked = jnp.concatenate(parts, axis=0)
                along_y.append(jnp.dot(band_y[...], stacked, preferred_element_type=F32))
        along_z = jnp.dot(split[...], band_z[...], preferred_element_type=F32)
        for k in range(BATCH):
            for s in range(shots):
                rows = (k * shots + s) * width_y
                both = along_z[rows : rows + width_y, :] + along_y[k * shots + s]
                flat[s, BATCH * batch + k] = both * (1.0 / 5040.0)
        return carry

    lax.fori_loop(0, flat.shape[1] // BATCH, layers, 0)


def laplace_line(field, flat, s, row, z):
    width_x = flat.shape[1]
    line = [field[s, x, row, z] for x in range(width_x)]
    for x in range(width_x):
        total = 3.0 * COEFS[0] * line[x] + flat[s, x, row, z]
        for r in range(1, 5):
            near = [line[i] for i in (x - r, x + r) if 0 <= i < width_x]
            if near:
                total = total + COEFS[r] * (near[0] if len(near) == 1 else near[0] + near[1])
        yield x, line[x], total


def place(cells, rows_y, width_x, width_y):
    bits = rows_y.bit_length() - 1
    x = lax.shift_right_logical(cells, bits) - lax.axis_index("gx") * width_x
    y = (cells & (rows_y - 1)) - lax.axis_index("gy") * width_y
    return x, y


def forward_march(offset, rows_y, step_ref, src_ref, wave_ref, u, u_old, a, cour, *refs):
    if offset:
        band_y, band_z, image_in, u_out, image, prior, *refs = refs
    else:
        u_out, image, band_y, band_z, *refs = refs
    split, flat, *old, sems = refs
    shots, width_x, width_y, depth = u.shape
    copies = Copies(sems)
    moves = [copies.start(u, prior) if offset else copies.start(u_old, old[0])]
    u_old = u_old if offset else old[0]
    if not offset:
        make_bands(band_y, band_z)
    plane_stencil(lambda s, x: u[s, x], shots, band_y, band_z, split, flat)
    if not offset:
        moves.pop().wait()

    def tiles(t, carry):
        row = pl.ds(pl.multiple_of(8 * t, 8), 8)
        for h, z in enumerate(halves(depth)):
            for s in range(shots):
                for x, center, lap in laplace_line(u, flat, s, row, z):
                    mass = cour[x, row, z] * cour[x, row, z]
                    u_out[s, x, row, z] = 2.0 * center - u_old[s, x, row, z] + mass * lap
                    term = a[s, x, row, z] * lap
                    if s:
                        image[h, x, row, :] = image[h, x, row, :] + term
                    else:
                        image[h, x, row, :] = image_in[h, x, row, :] + term if offset else term
        return carry

    lax.fori_loop(0, width_y // 8, tiles, 0)
    lane, sub = iota(1), iota(0)
    for s in range(shots):
        at_x, at_y = place(src_ref[s], rows_y, width_x, width_y)

        @pl.when((at_x >= 0) & (at_x < width_x) & (at_y >= 0) & (at_y < width_y))
        def _():
            row = pl.ds(pl.multiple_of((at_y // 8) * 8, 8), 8)
            speed = cour[at_x, row, 0:128]
            hit = (sub == at_y % 8) & (lane == SRC_DEPTH)
            added = jnp.where(hit, speed * speed * wave_ref[s, step_ref[s] - offset], 0.0)
            u_out[s, at_x, row, 0:128] = u_out[s, at_x, row, 0:128] + added

    for move in moves:
        move.wait()


def adjoint_march(offset, rows_y, step_ref, rec_hbm, trace_hbm, a, a_old, cour, band_y, band_z, *refs):
    done, refs = (refs[0], refs[1:]) if offset else (None, refs)
    a_out, *refs = refs
    outs, refs = (refs[:2], refs[2:]) if offset else ((), refs)
    split, flat, scaled, trace, rec_ref, *old, sems = refs
    shots, width_x, width_y, depth = a.shape
    copies = Copies(sems)
    loads = [copies.start(rec_hbm, rec_ref)]
    for s in range(shots):
        block = pl.multiple_of(((step_ref[s] - offset) // 8) * 8, 8)
        loads.append(copies.start(trace_hbm.at[s, pl.ds(block, 8), :], trace.at[s]))
    if offset:
        moves = [copies.start(src, dst) for src, dst in zip((a, done), outs)]
    else:
        moves = [copies.start(a_old, old[0])]
        a_old = old[0]

    def scale(s, x):
        block = cour[x] * cour[x] * a[s, x]
        scaled[s, x] = block
        return block

    plane_stencil(scale, shots, band_y, band_z, split, flat)
    if not offset:
        moves.pop().wait()

    def tiles(t, carry):
        row = pl.ds(pl.multiple_of(8 * t, 8), 8)
        for z in halves(depth):
            for s in range(shots):
                for x, _, lap in laplace_line(scaled, flat, s, row, z):
                    a_out[s, x, row, z] = 2.0 * a[s, x, row, z] - a_old[s, x, row, z] + lap
        return carry

    lax.fori_loop(0, width_y // 8, tiles, 0)
    for load in loads:
        load.wait()
    for s in range(shots):
        moment = step_ref[s] - offset
        pick = lax.broadcasted_iota(jnp.int32, trace.shape[1:], 0) == moment % 8
        values = jnp.sum(jnp.where(pick, trace[s], 0.0), axis=0, keepdims=True)
        at_x, at_y = place(rec_ref[s : s + 1, :], rows_y, width_x, width_y)
        count = at_x.shape[1]
        hot_x = lax.broadcasted_iota(jnp.int32, (width_x, count), 0) == at_x
        hot_y = lax.broadcasted_iota(jnp.int32, (width_y, count), 0) == at_y
        spread = [jnp.where(hot_y, part.astype(F32), 0.0).astype(BF16) for part in three_parts(values)]
        planes = lax.dot_general(
            jnp.concatenate(spread, axis=0),
            jnp.where(hot_x, 1.0, 0.0).astype(BF16),
            (((1,), (1,)), ((), ())),
            preferred_element_type=F32,
        )
        plane = planes[0:width_y] + planes[width_y : 2 * width_y] + planes[2 * width_y :]
        depth_mask = lax.broadcasted_iota(jnp.int32, (width_y, 128), 1) == REC_DEPTH
        for x in range(width_x):
            added = jnp.where(depth_mask, plane[:, x : x + 1], 0.0)
            a_out[s, x, :, 0:128] = a_out[s, x, :, 0:128] + added
    for move in moves:
        move.wait()


def packed(load, target, x):
    lane = lax.broadcasted_iota(jnp.int32, (16, 128), 1)
    block = load(target // 2, x)
    top, bottom = block[0:16, :], block[16:32, :]
    front = jnp.where(lane < 64, top, pltpu.roll(bottom, 64, 1))
    back = jnp.where(lane < 64, pltpu.roll(top, 64, 1), bottom)
    return jnp.where(target % 2 == 0, front, back)


def add_edges(hy, hx, field_at, out, cour, forward, a, image):
    shots, width_x, width_y, depth = out.shape
    sub = iota(0)
    even = even_on("gy")
    has_below, has_above = has_neighbour("gy", -1), has_neighbour("gy", 1)

    def coef(values):
        row = jnp.zeros((8, 128), F32)
        for j, v in values:
            row = jnp.where(sub == j, v, row)
        return row

    low_coef = [None] + [coef([(j, COEFS[r]) for j in range(4) if j < r]) for r in range(1, 5)]
    high_coef = [None] + [coef([(p, COEFS[r]) for p in range(4, 8) if p >= 8 - r]) for r in range(1, 5)]

    def turned(v, shift):
        return v if shift % 8 == 0 else pltpu.roll(v, shift % 8, 0)

    def rows(x, carry):
        for h, z in enumerate(halves(depth)):
            first = hy[0][field_at, x, :, z]
            second = hy[1][field_at, x, :, z] if len(hy) > 1 else jnp.zeros_like(first)
            below = jnp.where(has_below, jnp.where(even, second, first), 0.0)
            above = jnp.where(has_above, jnp.where(even, first, second), 0.0)
            for side in range(2):
                row = slice(0, 8) if side == 0 else slice(width_y - 8, width_y)
                for s in range(shots):
                    lap = None
                    for r in range(1, 5):
                        if side == 0:
                            part = low_coef[r] * turned(below, r - 4 + 4 * s)
                        else:
                            part = high_coef[r] * turned(above, 8 - r - 4 * s)
                        lap = part if lap is None else lap + part
                    if forward:
                        mass = cour[x, row, z] * cour[x, row, z]
                        out[s, x, row, z] = out[s, x, row, z] + mass * lap
                        image[h, x, row, :] = image[h, x, row, :] + a[s, x, row, z] * lap
                    else:
                        out[s, x, row, z] = out[s, x, row, z] + lap
        return carry

    lax.fori_loop(0, width_x, rows, 0, unroll=4)
    for turn, ref in enumerate(hx):
        toward = jnp.where(even_on("gx"), 1, -1) * (1 if turn == 0 else -1)
        whole = turn == 0 and lax.axis_size("gx") % 2 == 0
        for j in range(4):
            x = edge_layer("gx", width_x, turn, j)
            for h, z in enumerate(halves(depth)):
                for s in range(shots):
                    lap = None
                    for k in range(4 - j):
                        part = COEFS[j + k + 1] * ref[field_at, s, k, :, z]
                        lap = part if lap is None else lap + part
                    if not whole:
                        lap = jnp.where(has_neighbour("gx", toward), lap, 0.0)
                    if forward:
                        mass = cour[x, :, z] * cour[x, :, z]
                        out[s, x, :, z] = out[s, x, :, z] + mass * lap
                        image[h, x] = image[h, x] + a[s, x, :, z] * lap
                    else:
                        out[s, x, :, z] = out[s, x, :, z] + lap


def write_sends(turns_y, sends, out, cour):
    shots, width_x, width_y, depth = out.shape
    ys, xs = sends[:turns_y], sends[turns_y:]

    def line(x, carry):
        for z in halves(depth):
            tiles = []
            for row in (slice(0, 8), slice(width_y - 8, width_y)):
                for s in range(shots):
                    tile = out[s, x, row, z]
                    tiles.append(tile if cour is None else cour[x, row, z] * cour[x, row, z] * tile)
            write_y_sends(ys, 0, x, z, *tiles)
        return carry

    lax.fori_loop(0, width_x, line, 0, unroll=4)
    for turn, ref in enumerate(xs):
        for k in range(4):
            x = edge_layer("gx", width_x, turn, k)
            for s in range(shots):
                ref[0, s, k] = out[s, x] if cour is None else cour[x] * cour[x] * out[s, x]


def forward_edge(turns_x, turns_y, last, *refs):
    hy, hx, refs = refs[:turns_y], refs[turns_y : turns_y + turns_x], refs[turns_y + turns_x :]
    a, cour, *refs = refs
    u_out, image, *sends = refs[2 if last else 3 :]
    add_edges(hy, hx, 0, u_out, cour, True, a, image)
    if not last:
        write_sends(turns_y, sends, u_out, None)
        return
    me = lax.axis_index("shot")
    lane = lax.broadcasted_iota(jnp.int32, (16, 128), 1)

    def parts(x, carry):
        pairs = []
        for h in range(2):
            top, bottom = image[h, x, 0:16, :], image[h, x, 16:32, :]
            front = jnp.where(lane < 64, top, pltpu.roll(bottom, 64, 1))
            back = jnp.where(lane < 64, pltpu.roll(top, 64, 1), bottom)
            odd = me % 2 == 1
            pairs.append((jnp.where(odd, back, front), jnp.where(odd, front, back)))
        for k, ref in enumerate(sends):
            ref[x] = jnp.where(me // 2 == 1, pairs[1 - k // 2][k % 2], pairs[k // 2][k % 2])
        return carry

    lax.fori_loop(0, u_out.shape[1], parts, 0, unroll=4)


def adjoint_edge(turns_x, turns_y, field_at, last, *refs):
    hy, hx, refs = refs[:turns_y], refs[turns_y : turns_y + turns_x], refs[turns_y + turns_x :]
    cour, _, a_out, *refs = refs
    add_edges(hy, hx, field_at, a_out, cour, False, None, None)
    if not last:
        write_sends(turns_y, refs, a_out, cour)
        return
    final, sem = refs
    copy = pltpu.make_async_copy(a_out, final, sem.at[0])
    copy.start()
    copy.wait()


def finish(scale, cour, own, first, second, third, out):
    me = lax.axis_index("shot")

    def line(x, carry):
        speed = packed(lambda h, x: jnp.where(h == 0, cour[x, :, 0:128], cour[x, :, 128:256]), me, x)
        total = own[x] + first[x] + second[x] + third[x]
        value = 2.0 * speed * total / scale
        out[x, 0:16, :] = value[:, 0:64]
        out[x, 16:32, :] = value[:, 64:128]
        return carry

    lax.fori_loop(0, out.shape[0], line, 0, unroll=4)


def call(body, outs, scratch, in_specs, args, cost, aliases=None, out_specs=None, limit=24 << 20):
    return pl.pallas_call(
        body,
        out_shape=outs,
        in_specs=in_specs,
        out_specs=out_specs or [VMEM] * len(outs),
        scratch_shapes=scratch,
        input_output_aliases=aliases or {},
        compiler_params=pltpu.CompilerParams(vmem_limit_bytes=limit),
        cost_estimate=pl.CostEstimate(flops=cost, bytes_accessed=cost, transcendentals=0),
    )(*args)


def shards(
    fwd_now, fwd_next, adj_now, adj_next, courant, wavelet, traces, src_cells, rec_cells, step_index
):
    shots, width_x, width_y, depth = fwd_now.shape
    groups = lax.axis_size("shot")
    rows_y = width_y * lax.axis_size("gy")
    assert rows_y & (rows_y - 1) == 0 and depth == 256 and groups == 4 and width_y == 32 and shots == 2
    perms_x, perms_y = pair_permutes("gx", "gy"), pair_permutes("gy", "gx")
    turns_x, turns_y = len(perms_x), len(perms_y)

    def shape(*dims):
        return jax.ShapeDtypeStruct(dims, F32)

    def swap(sends, perms):
        halos = []
        for send, perm in zip(sends, perms):
            halos.append(lax.ppermute(send, ("gx", "gy"), perm))
        return halos

    wave = shape(*fwd_now.shape)
    strip = shape(2, width_x, width_y, 128)
    y_send, x_rows = (width_x, 8, depth), (shots, 4, width_y, depth)
    y_rows = (shots, width_x, 8, depth)
    first_y = call(
        first_y_sends,
        [shape(2, *y_send)] * turns_y,
        [pltpu.VMEM(y_rows, F32)] * 4 + [pltpu.VMEM(y_rows[1:], F32)] * 2 + [pltpu.SemaphoreType.DMA((6,))],
        [HBM] * 3,
        (in_hbm(fwd_now), in_hbm(adj_now), in_hbm(courant)),
        1 << 20,
    )
    hy_u = hy_a = swap(first_y, perms_y)
    first_x = call(
        first_x_sends,
        [shape(2, *x_rows)] * turns_x,
        [],
        [VMEM] * 3,
        (fwd_now, adj_now, courant),
        1 << 20,
    )
    hx_u = hx_a = swap(first_x, perms_x)
    next_sends = [shape(1, *y_send)] * turns_y + [shape(1, *x_rows)] * turns_x
    bands = [jax.ShapeDtypeStruct((width_y, 3 * width_y), BF16), jax.ShapeDtypeStruct((3 * depth, depth), BF16)]
    stencil = [
        pltpu.VMEM((BATCH * shots * width_y, 3 * depth), BF16),
        pltpu.VMEM(fwd_now.shape, F32),
    ]
    sample = [pltpu.VMEM((shots, 8, traces.shape[-1]), F32), pltpu.VMEM(rec_cells.shape, jnp.int32)]
    u_now, u_next, a_now, a_next = fwd_now, fwd_next, adj_now, adj_next
    image = None
    for offset in range(STEPS):
        last = offset == STEPS - 1
        old_spec = VMEM if offset else HBM
        old_rows = [] if offset else [pltpu.VMEM(fwd_now.shape, F32)]
        old = u_next if offset else in_hbm(u_next)
        u_prev, image, *rest = call(
            functools.partial(forward_march, offset, rows_y),
            [wave, strip] + ([wave] if offset else bands),
            stencil + old_rows + [pltpu.SemaphoreType.DMA((1,))],
            [SMEM] * 3 + [VMEM, old_spec] + [VMEM] * (2 + 3 * offset),
            (step_index, src_cells, wavelet, u_now, old, a_now, courant) + ((*bands, image) if offset else ()),
            8 << 20,
            out_specs=[VMEM] * 2 + ([HBM] if offset else [VMEM] * 2),
        )
        if offset:
            forward_prior = rest[0]
        else:
            bands = rest

        def run_forward_edge(u_prev, image, *after):
            args = (*hy_u, *hx_u, a_now, courant, *after, in_vmem(u_prev), in_vmem(image))
            return call(
                functools.partial(forward_edge, turns_x, turns_y, last),
                [wave, strip] + ([shape(width_x, 16, 128)] * groups if last else next_sends),
                [],
                [VMEM] * len(args),
                args,
                1 << 20,
                {len(args) - 2: 0, len(args) - 1: 1},
            )

        def run_adjoint_march(*done):
            old = a_next if offset else in_hbm(a_next)
            return call(
                functools.partial(adjoint_march, offset, rows_y),
                [wave] * (1 + 2 * offset),
                stencil + stencil[1:] + sample + old_rows + [pltpu.SemaphoreType.DMA((shots + 3,))],
                [SMEM] + [HBM] * 2 + [VMEM, old_spec] + [VMEM] * (3 + offset),
                (step_index, in_hbm(rec_cells), in_hbm(traces), a_now, old, courant, *bands)
                + tuple(in_vmem(d) for d in done),
                8 << 20,
                out_specs=[VMEM] + [HBM] * (2 * offset),
            )

        if offset:
            u_prev, image, *u_sends = run_forward_edge(u_prev, image)
            a_prev, *rest = run_adjoint_march(u_prev)
        else:
            a_prev, *rest = run_adjoint_march()
            u_prev, image, *u_sends = run_forward_edge(u_prev, image, a_prev)
        if last:
            parts = [u_sends[0]]
            for k in (3, 1, 2):
                parts.append(lax.ppermute(u_sends[k], "shot", [(i, i ^ k) for i in range(groups)]))
        else:
            hy_u = swap(u_sends[:turns_y], perms_y)
            hx_u = swap(u_sends[turns_y:], perms_x)
        if offset:
            adjoint_prior, forward_start = rest
        args = (*hy_a, *hx_a, courant, in_vmem(a_prev))
        a_prev, *a_sends = call(
            functools.partial(adjoint_edge, turns_x, turns_y, 0 if offset else 1, last),
            [wave] + ([wave] if last else next_sends),
            [pltpu.SemaphoreType.DMA((1,))] if last else [],
            [VMEM] * len(args),
            args,
            1 << 20,
            {len(args) - 1: 0},
            out_specs=[VMEM, HBM] if last else None,
        )
        if last:
            (adjoint_start,) = a_sends
        else:
            hy_a = swap(a_sends[:turns_y], perms_y)
            hx_a = swap(a_sends[turns_y:], perms_x)
        u_next, u_now = u_now, u_prev
        a_next, a_now = a_now, a_prev
    (gradient,) = call(
        functools.partial(finish, float(shots * groups * STEPS)),
        [shape(width_x, width_y, depth // groups)],
        [],
        [VMEM] * 5,
        (courant, *parts),
        1 << 20,
    )
    return (forward_prior, forward_start, adjoint_prior, adjoint_start, gradient)


def solution(mesh):
    fields = P("shot", "gx", "gy", None)
    in_specs = (fields,) * 4 + (
        P("gx", "gy", None),
        P("shot", None),
        P("shot", None, None),
        P("shot"),
        P("shot", None),
        P("shot"),
    )
    out_specs = (fields,) * 4 + (P("gx", "gy", "shot"),)
    return jax.shard_map(shards, mesh=mesh, in_specs=in_specs, out_specs=out_specs, check_vma=False)
```

```python
import functools

import jax
import jax.numpy as jnp
from jax import lax
from jax.experimental import pallas as pl
from jax.experimental.pallas import tpu as pltpu
from jax.sharding import PartitionSpec as P


STEPS = 2
SRC_DEPTH = 4
REC_DEPTH = 6
COEFS = (-205.0 / 72.0, 8.0 / 5.0, -1.0 / 5.0, 8.0 / 315.0, -1.0 / 560.0)
F32 = jnp.float32
BF16 = jnp.bfloat16
VMEM = pl.BlockSpec(memory_space=pltpu.VMEM)
SMEM = pl.BlockSpec(memory_space=pltpu.SMEM)
HBM = pl.BlockSpec(memory_space=pltpu.HBM)


def iota(dim):
    return lax.broadcasted_iota(jnp.int32, (8, 128), dim)


def even_on(axis):
    return lax.axis_index(axis) % 2 == 0


def pair_permutes(axis, other):
    count, across = lax.axis_size(axis), lax.axis_size(other)
    perms = []

    def at(i, j):
        return i * across + j if axis == "gx" else j * count + i

    for first in (0, 1):
        pairs = [(i, i + 1) for i in range(first, count - 1, 2)]
        if not pairs:
            continue
        left = set(range(count)) - {i for pair in pairs for i in pair}
        perm = [(at(a, j), at(b, j)) for a, b in pairs for j in range(across)]
        perm += [(b, a) for a, b in perm]
        if across % 2 == 0:
            perm += [(at(i, j), at(i, j ^ 1)) for i in sorted(left) for j in range(across)]
        perms.append(perm)
    return perms


def has_neighbour(axis, step):
    at = lax.axis_index(axis) + step
    return (at >= 0) & (at < lax.axis_size(axis))


def edge_layer(axis, width, turn, k):
    high = even_on(axis) if turn == 0 else jnp.logical_not(even_on(axis))
    return jnp.where(high, width - 1 - k, k)


def in_hbm(x):
    return pltpu.with_memory_space_constraint(x, pltpu.HBM)


def in_vmem(x):
    return pltpu.with_memory_space_constraint(x, pltpu.VMEM)


def halves(depth):
    return [slice(h * 128, h * 128 + 128) for h in range(depth // 128)]


def write_y_sends(sends, at, x, z, low_0, low_1, high_0, high_1):
    sub = iota(0)
    low = jnp.where(sub < 4, low_0, pltpu.roll(low_1, 4, 0))
    high = jnp.where(sub < 4, pltpu.roll(high_0, 4, 0), high_1)
    even = even_on("gy")
    for turn, ref in enumerate(sends):
        pick = even if turn == 0 else jnp.logical_not(even)
        ref[at, x, :, z] = jnp.where(pick, high, low)


class Copies:
    def __init__(self, sems):
        self.sems, self.count = sems, 0

    def start(self, src, dst):
        copy = pltpu.make_async_copy(src, dst, self.sems.at[self.count])
        copy.start()
        self.count += 1
        return copy


def first_y_sends(u_hbm, a_hbm, c_hbm, *refs):
    *ys, u_low, u_high, a_low, a_high, c_low, c_high, sems = refs
    forward, adjoint = ys[: len(ys) // 2], ys[len(ys) // 2 :]
    _, width_x, width_y, depth = u_hbm.shape
    copies = Copies(sems)
    waits = []
    for src, low, high in ((u_hbm, u_low, u_high), (a_hbm, a_low, a_high)):
        waits.append(copies.start(src.at[:, :, 0:8, :], low))
        waits.append(copies.start(src.at[:, :, width_y - 8 : width_y, :], high))
    waits.append(copies.start(c_hbm.at[:, 0:8, :], c_low))
    waits.append(copies.start(c_hbm.at[:, width_y - 8 : width_y, :], c_high))
    for wait in waits:
        wait.wait()

    def line(x, carry):
        for z in halves(depth):
            low = c_low[x, :, z] * c_low[x, :, z]
            high = c_high[x, :, z] * c_high[x, :, z]
            write_y_sends(forward, 0, x, z, *(ref[s, x, :, z] for ref in (u_low, u_high) for s in range(2)))
            write_y_sends(
                adjoint,
                0,
                x,
                z,
                *(m * ref[s, x, :, z] for m, ref in ((low, a_low), (high, a_high)) for s in range(2)),
            )
        return carry

    lax.fori_loop(0, width_x, line, 0, unroll=4)


def first_x_sends(u, a, cour, *xs):
    shots, width_x = u.shape[:2]
    for turn, ref in enumerate(xs):
        for k in range(4):
            x = edge_layer("gx", width_x, turn, k)
            for s in range(shots):
                ref[0, s, k] = u[s, x]
                ref[1, s, k] = cour[x] * cour[x] * a[s, x]


def band_of(apart):
    band = jnp.zeros(apart.shape, F32)
    for r in range(1, 5):
        band = jnp.where(apart == r, float(round(5040 * COEFS[r])), band)
    return band.astype(BF16)


def make_bands(band_y, band_z):
    rows, columns = band_y.shape
    at = lax.broadcasted_iota(jnp.int32, (rows, columns), 1) % rows
    band_y[...] = band_of(jnp.abs(at - lax.broadcasted_iota(jnp.int32, (rows, columns), 0)))
    depth = band_z.shape[1]
    at = lax.broadcasted_iota(jnp.int32, (depth, depth), 0)
    band = band_of(jnp.abs(at - lax.broadcasted_iota(jnp.int32, (depth, depth), 1)))
    for part in range(3):
        band_z[part * depth : part * depth + depth, :] = band


def three_parts(v):
    top = v.astype(BF16)
    rest = v - top.astype(F32)
    middle = rest.astype(BF16)
    return top, middle, (rest - middle.astype(F32)).astype(BF16)


BATCH = 16


def plane_stencil(block_of, shots, band_y, band_z, split, flat):
    depth = band_z.shape[1]
    width_y = band_y.shape[0]

    def layers(batch, carry):
        along_y = []
        for k in range(BATCH):
            for s in range(shots):
                parts = three_parts(block_of(s, BATCH * batch + k))
                rows = (k * shots + s) * width_y
                for part, value in enumerate(parts):
                    split[rows : rows + width_y, part * depth : part * depth + depth] = value
                stacked = jnp.concatenate(parts, axis=0)
                along_y.append(jnp.dot(band_y[...], stacked, preferred_element_type=F32))
        along_z = jnp.dot(split[...], band_z[...], preferred_element_type=F32)
        for k in range(BATCH):
            for s in range(shots):
                rows = (k * shots + s) * width_y
                both = along_z[rows : rows + width_y, :] + along_y[k * shots + s]
                flat[s, BATCH * batch + k] = both * (1.0 / 5040.0)
        return carry

    lax.fori_loop(0, flat.shape[1] // BATCH, layers, 0)


def laplace_line(field, flat, s, row, z):
    width_x = flat.shape[1]
    line = [field[s, x, row, z] for x in range(width_x)]
    for x in range(width_x):
        total = 3.0 * COEFS[0] * line[x] + flat[s, x, row, z]
        for r in range(1, 5):
            near = [line[i] for i in (x - r, x + r) if 0 <= i < width_x]
            if near:
                total = total + COEFS[r] * (near[0] if len(near) == 1 else near[0] + near[1])
        yield x, line[x], total


def place(cells, rows_y, width_x, width_y):
    bits = rows_y.bit_length() - 1
    x = lax.shift_right_logical(cells, bits) - lax.axis_index("gx") * width_x
    y = (cells & (rows_y - 1)) - lax.axis_index("gy") * width_y
    return x, y


def forward_march(offset, rows_y, step_ref, src_ref, wave_ref, u, u_old, a, cour, *refs):
    if offset:
        band_y, band_z, image_in, u_out, image, prior, *refs = refs
    else:
        u_out, image, band_y, band_z, *refs = refs
    split, flat, *old, sems = refs
    shots, width_x, width_y, depth = u.shape
    copies = Copies(sems)
    moves = [copies.start(u, prior) if offset else copies.start(u_old, old[0])]
    u_old = u_old if offset else old[0]
    if not offset:
        make_bands(band_y, band_z)
    plane_stencil(lambda s, x: u[s, x], shots, band_y, band_z, split, flat)
    if not offset:
        moves.pop().wait()

    def tiles(t, carry):
        row = pl.ds(pl.multiple_of(8 * t, 8), 8)
        for h, z in enumerate(halves(depth)):
            for s in range(shots):
                for x, center, lap in laplace_line(u, flat, s, row, z):
                    mass = cour[x, row, z] * cour[x, row, z]
                    u_out[s, x, row, z] = 2.0 * center - u_old[s, x, row, z] + mass * lap
                    term = a[s, x, row, z] * lap
                    if s:
                        image[h, x, row, :] = image[h, x, row, :] + term
                    else:
                        image[h, x, row, :] = image_in[h, x, row, :] + term if offset else term
        return carry

    lax.fori_loop(0, width_y // 8, tiles, 0)
    lane, sub = iota(1), iota(0)
    for s in range(shots):
        at_x, at_y = place(src_ref[s], rows_y, width_x, width_y)

        @pl.when((at_x >= 0) & (at_x < width_x) & (at_y >= 0) & (at_y < width_y))
        def _():
            row = pl.ds(pl.multiple_of((at_y // 8) * 8, 8), 8)
            speed = cour[at_x, row, 0:128]
            hit = (sub == at_y % 8) & (lane == SRC_DEPTH)
            added = jnp.where(hit, speed * speed * wave_ref[s, step_ref[s] - offset], 0.0)
            u_out[s, at_x, row, 0:128] = u_out[s, at_x, row, 0:128] + added

    for move in moves:
        move.wait()


def adjoint_march(offset, rows_y, step_ref, rec_hbm, trace_hbm, a, a_old, cour, band_y, band_z, *refs):
    done, refs = (refs[0], refs[1:]) if offset else (None, refs)
    a_out, *refs = refs
    outs, refs = (refs[:2], refs[2:]) if offset else ((), refs)
    split, flat, scaled, trace, rec_ref, *old, sems = refs
    shots, width_x, width_y, depth = a.shape
    copies = Copies(sems)
    loads = [copies.start(rec_hbm, rec_ref)]
    for s in range(shots):
        block = pl.multiple_of(((step_ref[s] - offset) // 8) * 8, 8)
        loads.append(copies.start(trace_hbm.at[s, pl.ds(block, 8), :], trace.at[s]))
    if offset:
        moves = [copies.start(src, dst) for src, dst in zip((a, done), outs)]
    else:
        moves = [copies.start(a_old, old[0])]
        a_old = old[0]

    def scale(s, x):
        block = cour[x] * cour[x] * a[s, x]
        scaled[s, x] = block
        return block

    plane_stencil(scale, shots, band_y, band_z, split, flat)
    if not offset:
        moves.pop().wait()

    def tiles(t, carry):
        row = pl.ds(pl.multiple_of(8 * t, 8), 8)
        for z in halves(depth):
            for s in range(shots):
                for x, _, lap in laplace_line(scaled, flat, s, row, z):
                    a_out[s, x, row, z] = 2.0 * a[s, x, row, z] - a_old[s, x, row, z] + lap
        return carry

    lax.fori_loop(0, width_y // 8, tiles, 0)
    for load in loads:
        load.wait()
    for s in range(shots):
        moment = step_ref[s] - offset
        pick = lax.broadcasted_iota(jnp.int32, trace.shape[1:], 0) == moment % 8
        values = jnp.sum(jnp.where(pick, trace[s], 0.0), axis=0, keepdims=True)
        at_x, at_y = place(rec_ref[s : s + 1, :], rows_y, width_x, width_y)
        count = at_x.shape[1]
        hot_x = lax.broadcasted_iota(jnp.int32, (width_x, count), 0) == at_x
        hot_y = lax.broadcasted_iota(jnp.int32, (width_y, count), 0) == at_y
        spread = [jnp.where(hot_y, part.astype(F32), 0.0).astype(BF16) for part in three_parts(values)]
        planes = lax.dot_general(
            jnp.concatenate(spread, axis=0),
            jnp.where(hot_x, 1.0, 0.0).astype(BF16),
            (((1,), (1,)), ((), ())),
            preferred_element_type=F32,
        )
        plane = planes[0:width_y] + planes[width_y : 2 * width_y] + planes[2 * width_y :]
        depth_mask = lax.broadcasted_iota(jnp.int32, (width_y, 128), 1) == REC_DEPTH
        for x in range(width_x):
            added = jnp.where(depth_mask, plane[:, x : x + 1], 0.0)
            a_out[s, x, :, 0:128] = a_out[s, x, :, 0:128] + added
    for move in moves:
        move.wait()


def packed(load, target, x):
    lane = lax.broadcasted_iota(jnp.int32, (16, 128), 1)
    block = load(target // 2, x)
    top, bottom = block[0:16, :], block[16:32, :]
    front = jnp.where(lane < 64, top, pltpu.roll(bottom, 64, 1))
    back = jnp.where(lane < 64, pltpu.roll(top, 64, 1), bottom)
    return jnp.where(target % 2 == 0, front, back)


def add_edges(hy, hx, field_at, out, cour, forward, a, image):
    shots, width_x, width_y, depth = out.shape
    sub = iota(0)
    even = even_on("gy")
    has_below, has_above = has_neighbour("gy", -1), has_neighbour("gy", 1)

    def coef(values):
        row = jnp.zeros((8, 128), F32)
        for j, v in values:
            row = jnp.where(sub == j, v, row)
        return row

    low_coef = [None] + [coef([(j, COEFS[r]) for j in range(4) if j < r]) for r in range(1, 5)]
    high_coef = [None] + [coef([(p, COEFS[r]) for p in range(4, 8) if p >= 8 - r]) for r in range(1, 5)]

    def turned(v, shift):
        return v if shift % 8 == 0 else pltpu.roll(v, shift % 8, 0)

    def rows(x, carry):
        for h, z in enumerate(halves(depth)):
            first = hy[0][0, x, :, z]
            second = hy[1][0, x, :, z] if len(hy) > 1 else jnp.zeros_like(first)
            below = jnp.where(has_below, jnp.where(even, second, first), 0.0)
            above = jnp.where(has_above, jnp.where(even, first, second), 0.0)
            for side in range(2):
                row = slice(0, 8) if side == 0 else slice(width_y - 8, width_y)
                for s in range(shots):
                    lap = None
                    for r in range(1, 5):
                        if side == 0:
                            part = low_coef[r] * turned(below, r - 4 + 4 * s)
                        else:
                            part = high_coef[r] * turned(above, 8 - r - 4 * s)
                        lap = part if lap is None else lap + part
                    if forward:
                        mass = cour[x, row, z] * cour[x, row, z]
                        out[s, x, row, z] = out[s, x, row, z] + mass * lap
                        image[h, x, row, :] = image[h, x, row, :] + a[s, x, row, z] * lap
                    else:
                        out[s, x, row, z] = out[s, x, row, z] + lap
        return carry

    lax.fori_loop(0, width_x, rows, 0, unroll=4)
    for turn, ref in enumerate(hx):
        toward = jnp.where(even_on("gx"), 1, -1) * (1 if turn == 0 else -1)
        whole = turn == 0 and lax.axis_size("gx") % 2 == 0
        for j in range(4):
            x = edge_layer("gx", width_x, turn, j)
            for h, z in enumerate(halves(depth)):
                for s in range(shots):
                    lap = None
                    for k in range(4 - j):
                        part = COEFS[j + k + 1] * ref[field_at, s, k, :, z]
                        lap = part if lap is None else lap + part
                    if not whole:
                        lap = jnp.where(has_neighbour("gx", toward), lap, 0.0)
                    if forward:
                        mass = cour[x, :, z] * cour[x, :, z]
                        out[s, x, :, z] = out[s, x, :, z] + mass * lap
                        image[h, x] = image[h, x] + a[s, x, :, z] * lap
                    else:
                        out[s, x, :, z] = out[s, x, :, z] + lap


def write_sends(turns_y, sends, out, cour):
    shots, width_x, width_y, depth = out.shape
    ys, xs = sends[:turns_y], sends[turns_y:]

    def line(x, carry):
        for z in halves(depth):
            tiles = []
            for row in (slice(0, 8), slice(width_y - 8, width_y)):
                for s in range(shots):
                    tile = out[s, x, row, z]
                    tiles.append(tile if cour is None else cour[x, row, z] * cour[x, row, z] * tile)
            write_y_sends(ys, 0, x, z, *tiles)
        return carry

    lax.fori_loop(0, width_x, line, 0, unroll=4)
    for turn, ref in enumerate(xs):
        for k in range(4):
            x = edge_layer("gx", width_x, turn, k)
            for s in range(shots):
                ref[0, s, k] = out[s, x] if cour is None else cour[x] * cour[x] * out[s, x]


def forward_edge(turns_x, turns_y, last, *refs):
    hy, hx, refs = refs[:turns_y], refs[turns_y : turns_y + turns_x], refs[turns_y + turns_x :]
    a, cour, *refs = refs
    u_out, image, *sends = refs[2 if last else 3 :]
    add_edges(hy, hx, 0, u_out, cour, True, a, image)
    if not last:
        write_sends(turns_y, sends, u_out, None)
        return
    me = lax.axis_index("shot")
    lane = lax.broadcasted_iota(jnp.int32, (16, 128), 1)

    def parts(x, carry):
        pairs = []
        for h in range(2):
            top, bottom = image[h, x, 0:16, :], image[h, x, 16:32, :]
            front = jnp.where(lane < 64, top, pltpu.roll(bottom, 64, 1))
            back = jnp.where(lane < 64, pltpu.roll(top, 64, 1), bottom)
            odd = me % 2 == 1
            pairs.append((jnp.where(odd, back, front), jnp.where(odd, front, back)))
        for k, ref in enumerate(sends):
            ref[x] = jnp.where(me // 2 == 1, pairs[1 - k // 2][k % 2], pairs[k // 2][k % 2])
        return carry

    lax.fori_loop(0, u_out.shape[1], parts, 0, unroll=4)


def adjoint_edge(turns_x, turns_y, field_at, last, *refs):
    hy, hx, refs = refs[:turns_y], refs[turns_y : turns_y + turns_x], refs[turns_y + turns_x :]
    cour, _, a_out, *refs = refs
    add_edges(hy, hx, field_at, a_out, cour, False, None, None)
    if not last:
        write_sends(turns_y, refs, a_out, cour)
        return
    final, sem = refs
    copy = pltpu.make_async_copy(a_out, final, sem.at[0])
    copy.start()
    copy.wait()


def finish(scale, cour, own, first, second, third, out):
    me = lax.axis_index("shot")

    def line(x, carry):
        speed = packed(lambda h, x: jnp.where(h == 0, cour[x, :, 0:128], cour[x, :, 128:256]), me, x)
        total = own[x] + first[x] + second[x] + third[x]
        value = 2.0 * speed * total / scale
        out[x, 0:16, :] = value[:, 0:64]
        out[x, 16:32, :] = value[:, 64:128]
        return carry

    lax.fori_loop(0, out.shape[0], line, 0, unroll=4)


def call(body, outs, scratch, in_specs, args, cost, aliases=None, out_specs=None, limit=24 << 20):
    return pl.pallas_call(
        body,
        out_shape=outs,
        in_specs=in_specs,
        out_specs=out_specs or [VMEM] * len(outs),
        scratch_shapes=scratch,
        input_output_aliases=aliases or {},
        compiler_params=pltpu.CompilerParams(vmem_limit_bytes=limit),
        cost_estimate=pl.CostEstimate(flops=cost, bytes_accessed=cost, transcendentals=0),
    )(*args)


def shards(
    fwd_now, fwd_next, adj_now, adj_next, courant, wavelet, traces, src_cells, rec_cells, step_index
):
    shots, width_x, width_y, depth = fwd_now.shape
    groups = lax.axis_size("shot")
    rows_y = width_y * lax.axis_size("gy")
    assert rows_y & (rows_y - 1) == 0 and depth == 256 and groups == 4 and width_y == 32 and shots == 2
    perms_x, perms_y = pair_permutes("gx", "gy"), pair_permutes("gy", "gx")
    turns_x, turns_y = len(perms_x), len(perms_y)

    def shape(*dims):
        return jax.ShapeDtypeStruct(dims, F32)

    def swap(sends, perms):
        halos = []
        for send, perm in zip(sends, perms):
            halos.append(lax.ppermute(send, ("gx", "gy"), perm))
        return halos

    wave = shape(*fwd_now.shape)
    strip = shape(2, width_x, width_y, 128)
    y_send, x_rows = (width_x, 8, depth), (shots, 4, width_y, depth)
    y_rows = (shots, width_x, 8, depth)
    first_y = call(
        first_y_sends,
        [shape(1, *y_send)] * (2 * turns_y),
        [pltpu.VMEM(y_rows, F32)] * 4 + [pltpu.VMEM(y_rows[1:], F32)] * 2 + [pltpu.SemaphoreType.DMA((6,))],
        [HBM] * 3,
        (in_hbm(fwd_now), in_hbm(adj_now), in_hbm(courant)),
        1 << 20,
    )
    hy_u = swap(first_y[:turns_y], perms_y)
    hy_a = swap(first_y[turns_y:], perms_y)
    first_x = call(
        first_x_sends,
        [shape(2, *x_rows)] * turns_x,
        [],
        [VMEM] * 3,
        (fwd_now, adj_now, courant),
        1 << 20,
    )
    hx_u = hx_a = swap(first_x, perms_x)
    next_sends = [shape(1, *y_send)] * turns_y + [shape(1, *x_rows)] * turns_x
    bands = [jax.ShapeDtypeStruct((width_y, 3 * width_y), BF16), jax.ShapeDtypeStruct((3 * depth, depth), BF16)]
    stencil = [
        pltpu.VMEM((BATCH * shots * width_y, 3 * depth), BF16),
        pltpu.VMEM(fwd_now.shape, F32),
    ]
    sample = [pltpu.VMEM((shots, 8, traces.shape[-1]), F32), pltpu.VMEM(rec_cells.shape, jnp.int32)]
    u_now, u_next, a_now, a_next = fwd_now, fwd_next, adj_now, adj_next
    image = None
    for offset in range(STEPS):
        last = offset == STEPS - 1
        old_spec = VMEM if offset else HBM
        old_rows = [] if offset else [pltpu.VMEM(fwd_now.shape, F32)]
        old = u_next if offset else in_hbm(u_next)
        u_prev, image, *rest = call(
            functools.partial(forward_march, offset, rows_y),
            [wave, strip] + ([wave] if offset else bands),
            stencil + old_rows + [pltpu.SemaphoreType.DMA((1,))],
            [SMEM] * 3 + [VMEM, old_spec] + [VMEM] * (2 + 3 * offset),
            (step_index, src_cells, wavelet, u_now, old, a_now, courant) + ((*bands, image) if offset else ()),
            8 << 20,
            out_specs=[VMEM] * 2 + ([HBM] if offset else [VMEM] * 2),
        )
        if offset:
            forward_prior = rest[0]
        else:
            bands = rest

        def run_forward_edge(u_prev, image, *after):
            args = (*hy_u, *hx_u, a_now, courant, *after, in_vmem(u_prev), in_vmem(image))
            return call(
                functools.partial(forward_edge, turns_x, turns_y, last),
                [wave, strip] + ([shape(width_x, 16, 128)] * groups if last else next_sends),
                [],
                [VMEM] * len(args),
                args,
                1 << 20,
                {len(args) - 2: 0, len(args) - 1: 1},
            )

        def run_adjoint_march(*done):
            old = a_next if offset else in_hbm(a_next)
            return call(
                functools.partial(adjoint_march, offset, rows_y),
                [wave] * (1 + 2 * offset),
                stencil + stencil[1:] + sample + old_rows + [pltpu.SemaphoreType.DMA((shots + 3,))],
                [SMEM] + [HBM] * 2 + [VMEM, old_spec] + [VMEM] * (3 + offset),
                (step_index, in_hbm(rec_cells), in_hbm(traces), a_now, old, courant, *bands)
                + tuple(in_vmem(d) for d in done),
                8 << 20,
                out_specs=[VMEM] + [HBM] * (2 * offset),
            )

        if offset:
            u_prev, image, *u_sends = run_forward_edge(u_prev, image)
            a_prev, *rest = run_adjoint_march(u_prev)
        else:
            a_prev, *rest = run_adjoint_march()
            u_prev, image, *u_sends = run_forward_edge(u_prev, image, a_prev)
        if last:
            parts = [u_sends[0]]
            for k in (3, 1, 2):
                parts.append(lax.ppermute(u_sends[k], "shot", [(i, i ^ k) for i in range(groups)]))
        else:
            hy_u = swap(u_sends[:turns_y], perms_y)
            hx_u = swap(u_sends[turns_y:], perms_x)
        if offset:
            adjoint_prior, forward_start = rest
        args = (*hy_a, *hx_a, courant, in_vmem(a_prev))
        a_prev, *a_sends = call(
            functools.partial(adjoint_edge, turns_x, turns_y, 0 if offset else 1, last),
            [wave] + ([wave] if last else next_sends),
            [pltpu.SemaphoreType.DMA((1,))] if last else [],
            [VMEM] * len(args),
            args,
            1 << 20,
            {len(args) - 1: 0},
            out_specs=[VMEM, HBM] if last else None,
        )
        if last:
            (adjoint_start,) = a_sends
        else:
            hy_a = swap(a_sends[:turns_y], perms_y)
            hx_a = swap(a_sends[turns_y:], perms_x)
        u_next, u_now = u_now, u_prev
        a_next, a_now = a_now, a_prev
    (gradient,) = call(
        functools.partial(finish, float(shots * groups * STEPS)),
        [shape(width_x, width_y, depth // groups)],
        [],
        [VMEM] * 5,
        (courant, *parts),
        1 << 20,
    )
    return (forward_prior, forward_start, adjoint_prior, adjoint_start, gradient)


def solution(mesh):
    fields = P("shot", "gx", "gy", None)
    in_specs = (fields,) * 4 + (
        P("gx", "gy", None),
        P("shot", None),
        P("shot", None, None),
        P("shot"),
        P("shot", None),
        P("shot"),
    )
    out_specs = (fields,) * 4 + (P("gx", "gy", "shot"),)
    return jax.shard_map(shards, mesh=mesh, in_specs=in_specs, out_specs=out_specs, check_vma=False)
```
